128 devices in a mesh: region: 32 (over z, y, core), blk: 4 (over x).
Axes of the slice: x: 4, y: 4, z: 4, core: 2. Of those that a mesh axis runs over, the one named last changes fastest.
Arguments:
- jac_bus: float32 [1024, 8, 128, 128], P('region', 'blk'), may hold values from -0.1875 to 0.1875
- pattern: int32 [1024, 8], P(('region', 'blk')), may hold values from 0 to 23
- branch_weight: float32 [1024, 128], P(('region', 'blk')), may hold values from 0.2 to 5
- bus_diag: float32 [1024, 128], P(('region', 'blk')), may hold values from 0.3 to 3
- right_side: float32 [1024, 128], P(('region', 'blk')), may hold values from -8 to 8
Outputs:
- solution: float32 [1024, 128], P(('region', 'blk'))
- residual: float32 [1024, 128], P(('region', 'blk'))
The draws below stay inside these ranges and needn't reach their ends.
Inputs may be any that keep to these rules, and one draw needn't show every extreme that they name: pattern values below 8 name the region before the branch tile's region, those from 16 the region after it, with regions closed into a loop.
All inputs are finite; a program needn't handle non-finite values.
Results may differ from the reference program's by a relative error of at most 0.0003.
Values sent between devices are 32-bit elements; how exact they have to be, the bound alone decides.
A program may use at most 64 MiB of HBM per device.

```python
import math
import jax
import jax.numpy as jnp
from jax import lax

TILE = 128
SLOTS_BLK = 2
BR_TILES_DEV = 8
BUS_TILES_DEV = 8
ITERS = 12
SLOTS = 8
TILES = 1024
BTILES = 1024
N_REGION = 32
N_BLK = 4


def draw_right_side(key, part):
    position = jnp.arange(BTILES, dtype=jnp.float32)[:, None] / BTILES
    scale = 0.6 + 1.2 * position
    values = jax.random.normal(jax.random.fold_in(key, 5), (BTILES, TILE), jnp.float32) * scale
    return jnp.clip(values, -8.0, 8.0)


def set_ends(values, key, low, top_value):
    longest = values.shape.index(max(values.shape))
    spots = []
    for shift in (0, 1):
        where = [jax.random.randint(jax.random.fold_in(key, axis), (), 0, length) for axis, length in enumerate(values.shape)]
        where[longest] = (where[longest] + shift) % values.shape[longest]
        spots.append(tuple(where))
    return values.at[spots[0]].set(low).at[spots[1]].set(top_value)


def shard_levels(rng, shape, shards, low, top_value):
    level, own = 1.0, jax.random.fold_in(rng, 6)
    for dim, shards_of in shards:
        steps = jnp.exp(jax.random.uniform(jax.random.fold_in(own, dim), (shards_of,), jnp.float32, low / len(shards), top_value / len(shards)))
        level = level * jnp.repeat(steps, shape[dim] // shards_of).reshape([-1 if axis == dim else 1 for axis in range(len(shape))])
    return level


def centred(key, extent, deviation, limit, pieces=(), held_as=jnp.bfloat16):
    result = deviation * jax.random.normal(key, extent, jnp.float32)
    if pieces:
        result = result * shard_levels(key, extent, pieces, -0.22, 0.18)
    return jnp.clip(result, -limit, limit).astype(held_as)


def setup_inputs(seed: int = 0) -> dict:
    key_list = jax.random.split(jax.random.key(seed), 6)
    jac_bus = centred(key_list[0], (TILES, SLOTS, TILE, TILE), (TILE * BR_TILES_DEV * N_BLK * SLOTS_BLK // BUS_TILES_DEV) ** -0.5, 0.1875, ((0, 32), (1, 4)), jnp.float32)
    pattern = set_ends(jax.random.randint(key_list[1], (TILES, SLOTS), 0, 3 * BUS_TILES_DEV), jax.random.fold_in(key_list[1], 1), 0, (3 * BUS_TILES_DEV) - 1).astype(jnp.int32)
    branch_weight = jnp.clip(jnp.exp(math.log(5.0) - 3.218876 * jax.random.uniform(key_list[2], (TILES, TILE), jnp.float32) ** shard_levels(key_list[2], (TILES, TILE), ((0, 128),), -0.2, 0.2)), 0.2, 5.0)
    bus_diag = jnp.clip(jnp.exp(math.log(3.0) - 2.3025851 * jax.random.uniform(key_list[3], (BTILES, TILE), jnp.float32) ** shard_levels(key_list[3], (BTILES, TILE), ((0, 128),), -0.2, 0.2)), 0.3, 3.0)
    right_side = draw_right_side(jax.random.fold_in(key_list[5], 71), 0)
    return dict(jac_bus=jac_bus, pattern=pattern, branch_weight=branch_weight, bus_diag=bus_diag, right_side=right_side)


def column_tiles(pattern):
    tiles = jnp.arange(TILES, dtype=jnp.int32)
    region_of = tiles // (N_BLK * BR_TILES_DEV)
    group = jnp.arange(SLOTS, dtype=jnp.int32) // SLOTS_BLK
    offset = pattern // BUS_TILES_DEV
    within = pattern % BUS_TILES_DEV
    owner = (region_of[:, None] + offset - 1) % N_REGION
    return ((owner * N_BLK + group[None, :]) * BUS_TILES_DEV + within).astype(jnp.int32)


def apply_operator(jac_bus, index, branch_weight, bus_diag, vector):
    hp = lax.Precision.HIGHEST
    picked = vector[index]
    rows = jnp.einsum('tjab,tjb->ta', jac_bus, picked, precision=hp)
    weighted = branch_weight * rows
    back = jnp.einsum('tjab,ta->tjb', jac_bus, weighted, precision=hp)
    return bus_diag * vector + jnp.zeros_like(vector).at[index].add(back)


def reference(jac_bus, pattern, branch_weight, bus_diag, right_side):
    hp = lax.Precision.HIGHEST
    index = column_tiles(pattern)
    precond = bus_diag
    for slot in range(SLOTS):
        square = jac_bus[:, slot] * jac_bus[:, slot]
        contrib = jnp.einsum('tab,ta->tb', square, branch_weight, precision=hp)
        precond = precond.at[index[:, slot]].add(contrib)
    solution = jnp.zeros_like(right_side)
    residual = right_side
    scaled = residual / precond
    direction = scaled
    energy = jnp.sum(residual * scaled)
    for step in range(ITERS):
        image = apply_operator(jac_bus, index, branch_weight, bus_diag, direction)
        alpha = energy / jnp.sum(direction * image)
        solution = solution + alpha * direction
        residual = residual - alpha * image
        scaled = residual / precond
        fresh = jnp.sum(residual * scaled)
        direction = scaled + (fresh / energy) * direction
        energy = fresh
    return solution, residual
```

```python
import jax
import jax.numpy as jnp
from jax import lax
from jax.experimental import pallas as pl
from jax.experimental.pallas import tpu as pltpu
from jax.sharding import PartitionSpec as P

ITERS = 12
MESH = pl.DeviceIdType.MESH


def kernel(
    n_reg, n_blk,
    jac_hbm, pattern_ref, weight_ref, diag_ref, rhs_ref,
    sol_ref, res_ref,
    jac, pv, psm, wv, hsend, hbuf, oht, stage, back, uv, diag, xbuf, csend, rlo16, rhi16, rlo8, rhi8, dbuf,
    jsem, psem, gsend, grecv, hsend_sem, hrecv, xsend, xrecv, rsend, rrecv, dsend, drecv,
):
    reg = lax.axis_index("region")
    blk = lax.axis_index("blk")

    def region_at(k):
        return lax.rem(reg + k + n_reg, n_reg)

    def blk_at(k):
        return lax.rem(blk + k, n_blk)

    def to_blk(k):
        return (reg, blk_at(k))

    def to_reg(k):
        return (region_at(k), blk)

    def remote(src, dst, ssem, rsem, dev):
        return pltpu.make_async_remote_copy(
            src_ref=src, dst_ref=dst, send_sem=ssem, recv_sem=rsem,
            device_id=dev, device_id_type=MESH,
        )

    jcopies = [
        pltpu.make_async_copy(jac_hbm.at[pl.ds(8 * g, 8)], jac.at[pl.ds(8 * g, 8)], jsem.at[g])
        for g in range(4)
    ]
    for c in jcopies:
        c.start()

    barrier = pltpu.get_barrier_semaphore()
    for k in range(1, n_reg):
        pl.semaphore_signal(barrier, inc=1, device_id=to_reg(k), device_id_type=MESH)
    for k in range(1, n_blk):
        pl.semaphore_signal(barrier, inc=1, device_id=to_blk(k), device_id_type=MESH)

    pv[blk] = jnp.zeros((8, 128), jnp.int32)
    pv[blk, :, 0:8] = pattern_ref[...]
    wv[blk] = weight_ref[...]
    hsend[0:8] = diag_ref[...]
    hsend[8:16] = rhs_ref[...]
    stage[...] = jnp.zeros((128, 128), jnp.float32)
    back[...] = jnp.zeros((128, 128), jnp.float32)
    pl.semaphore_wait(barrier, n_reg - 1 + n_blk - 1)

    gcopies = []
    for k in range(1, n_blk):
        gcopies.append(remote(pv.at[blk], pv.at[blk], gsend.at[0, k], grecv.at[0, k], to_blk(k)))
        gcopies.append(remote(wv.at[blk], wv.at[blk], gsend.at[1, k], grecv.at[1, k], to_blk(k)))
    hcopies = [
        remote(hsend, hbuf.at[0], hsend_sem.at[0], hrecv.at[0], to_reg(1)),
        remote(hsend, hbuf.at[1], hsend_sem.at[1], hrecv.at[1], to_reg(-1)),
    ]
    for c in gcopies + hcopies:
        c.start()
    for c in gcopies:
        c.wait_recv()
    pcopy = pltpu.make_async_copy(pv, psm, psem)
    pcopy.start()

    lane = lax.broadcasted_iota(jnp.int32, (1, 128), 1)
    patf = pv[...].astype(jnp.float32).reshape(32, 128)
    lanes32 = lax.broadcasted_iota(jnp.int32, (32, 128), 1)
    for j in range(2):
        col = jnp.sum(jnp.where(lanes32 == 2 * blk + j, patf, 0.0), axis=1, keepdims=True)
        stage[32 * j : 32 * j + 32] = jnp.where(lanes32.astype(jnp.float32) == col, 1.0, 0.0)
    oht[...] = stage[...].T[0:32].astype(jnp.bfloat16)
    weight = wv[...].reshape(32, 128)

    def transposed_pad(rows):
        stage[0:32] = rows
        stage[32:64] = jnp.zeros((32, 128), jnp.float32)
        return stage[...].T

    def backward(rows, square, par):
        cols = transposed_pad(rows)
        for t in range(32):
            wc = jnp.broadcast_to(cols[:, t : t + 1], (128, 128))
            for j in range(2):
                tile = jac[t, j]
                term = tile * wc
                if square:
                    term = term * tile
                back[32 * j + t : 32 * j + t + 1] = jnp.sum(term, axis=0, keepdims=True)
        whole = back[...]
        high = whole.astype(jnp.bfloat16)
        rest = whole - high.astype(jnp.float32)
        mid = rest.astype(jnp.bfloat16)
        low = (rest - mid.astype(jnp.float32)).astype(jnp.bfloat16)
        hot = oht[...]

        def pick(piece):
            return jnp.dot(hot, piece, preferred_element_type=jnp.float32)

        total = pick(high) + (pick(mid) + pick(low))
        csend[par] = total[0:24]

    def r_copies(par):
        return [
            remote(csend.at[par, pl.ds(16, 8)], rlo8.at[par], rsend.at[par, 0], rrecv.at[par, 0], to_reg(2)),
            remote(csend.at[par, pl.ds(0, 8)], rhi8.at[par], rsend.at[par, 1], rrecv.at[par, 1], to_reg(-2)),
            remote(csend.at[par, pl.ds(8, 16)], rlo16.at[par], rsend.at[par, 2], rrecv.at[par, 2], to_reg(1)),
            remote(csend.at[par, pl.ds(0, 16)], rhi16.at[par], rsend.at[par, 3], rrecv.at[par, 3], to_reg(-1)),
        ]

    def r_sum(par):
        before = rlo8[par] + rlo16[par, 0:8] + csend[par, 0:8]
        own = rlo16[par, 8:16] + csend[par, 8:16] + rhi16[par, 0:8]
        after = csend[par, 16:24] + rhi16[par, 8:16] + rhi8[par]
        return jnp.concatenate([before, own, after], axis=0)

    for c in jcopies:
        c.wait()
    backward(weight, True, 0)
    copies = r_copies(0)
    for c in copies:
        c.start()
    pcopy.wait()
    for c in hcopies:
        c.wait_recv()
    for c in copies:
        c.wait_recv()
    diag[...] = jnp.concatenate([hbuf[0, 0:8], hsend[0:8], hbuf[1, 0:8]], axis=0)
    resid0 = jnp.concatenate([hbuf[0, 8:16], hsend[8:16], hbuf[1, 8:16]], axis=0)
    inv = 1.0 / (diag[...] + r_sum(0))
    for c in copies + gcopies + hcopies:
        c.wait_send()

    zeros8 = jnp.zeros((8, 128), jnp.float32)
    zeros24 = jnp.zeros((24, 128), jnp.float32)
    one = jnp.ones((1, 1), jnp.float32)

    def fold(first, second):
        both = jnp.where(lane < 64, first, second)
        rest = jnp.where(lane < 64, second, first)
        return both + pltpu.roll(rest, 64, 1)

    def step(i, carry):
        solution, direction, resid, along, gamma_old, alpha_old = carry
        par = lax.rem(i, 2)
        rpar = lax.rem(i + 1, 2)
        scaled = inv * resid
        uv[...] = scaled
        own_u = scaled[8:16]
        first = jnp.sum(own_u * resid[8:16], axis=0, keepdims=True)
        second = jnp.sum(own_u * own_u * diag[8:16], axis=0, keepdims=True)
        xbuf[par, blk, 32:33] = fold(first, second)

        lanes = lax.broadcasted_iota(jnp.int32, (128, 128), 1)
        acc = jnp.zeros((128, 128), jnp.float32)
        for t in range(32):
            x0 = uv[pl.ds(psm[t // 8, t % 8, 2 * blk], 1), :]
            x1 = uv[pl.ds(psm[t // 8, t % 8, 2 * blk + 1], 1), :]
            both = jac[t, 0] * x0 + jac[t, 1] * x1
            acc = jnp.where(lanes == t, jnp.sum(both, axis=1, keepdims=True), acc)
        xbuf[par, blk, 0:32] = acc.T[0:32]
        xcopies = [
            remote(xbuf.at[par, blk], xbuf.at[par, blk], xsend.at[par, k], xrecv.at[par, k], to_blk(k))
            for k in (2, 1, 3)
        ]
        for c in xcopies:
            c.start()
        for c in xcopies:
            c.wait_recv()
        rows = xbuf[par, 0, 0:32] + xbuf[par, 1, 0:32] + xbuf[par, 2, 0:32] + xbuf[par, 3, 0:32]
        scal = xbuf[par, 0, 32:33] + xbuf[par, 1, 32:33] + xbuf[par, 2, 32:33] + xbuf[par, 3, 32:33]
        weighted = weight * rows
        energy = jnp.sum(weighted * rows, axis=0, keepdims=True)
        dbuf[par, reg] = scal + fold(jnp.zeros((1, 128), jnp.float32), energy)
        dcopies = [
            remote(dbuf.at[par, reg], dbuf.at[par, reg], dsend.at[par], drecv.at[par], to_reg(k))
            for k in range(1, n_reg)
        ]
        for c in dcopies:
            c.start()
        backward(weighted, False, rpar)
        rcopies = r_copies(rpar)
        for c in rcopies:
            c.start()
        for c in rcopies:
            c.wait_recv()
        image = diag[...] * scaled + r_sum(rpar)
        others = dbuf.at[par, pl.ds(0, n_reg - 1)]
        dall = remote(others, others, dsend.at[par], drecv.at[par], to_reg(1))
        dall.wait_recv()
        sums = jnp.sum(dbuf[par].reshape(n_reg, 128), axis=0, keepdims=True)
        gamma = jnp.sum(jnp.where(lane < 64, sums, 0.0), axis=1, keepdims=True)
        delta = jnp.sum(jnp.where(lane < 64, 0.0, sums), axis=1, keepdims=True)
        begun = jnp.where(i == 0, 0.0, 1.0)
        beta = begun * gamma / gamma_old
        alpha = gamma / (delta - beta * gamma / alpha_old)
        direction = own_u + beta * direction
        along = image + beta * along
        solution = solution + alpha * direction
        resid = resid - alpha * along
        for c in xcopies + rcopies + [dall]:
            c.wait_send()
        return (solution, direction, resid, along, gamma, alpha)

    carry = lax.fori_loop(0, ITERS, step, (zeros8, zeros8, resid0, zeros24, one, one))
    sol_ref[...] = carry[0]
    res_ref[...] = carry[2][8:16]


def solution(mesh):
    n_reg, n_blk = mesh.shape["region"], mesh.shape["blk"]
    f32 = jnp.float32

    def body(jac_bus, pattern, branch_weight, bus_diag, right_side):
        vmem = pl.BlockSpec(memory_space=pltpu.VMEM)
        shape = jax.ShapeDtypeStruct((8, 128), f32)
        dma = pltpu.SemaphoreType.DMA

        def call(*args):
            return kernel(n_reg, n_blk, *args)

        return pl.pallas_call(
            call,
            out_shape=(shape, shape),
            in_specs=[pl.BlockSpec(memory_space=pl.ANY)] + [vmem] * 4,
            out_specs=(vmem, vmem),
            scratch_shapes=[
                pltpu.VMEM((32, 2, 128, 128), f32),
                pltpu.VMEM((4, 8, 128), jnp.int32),
                pltpu.SMEM((4, 8, 128), jnp.int32),
                pltpu.VMEM((4, 8, 128), f32),
                pltpu.VMEM((16, 128), f32),
                pltpu.VMEM((2, 16, 128), f32),
                pltpu.VMEM((32, 128), jnp.bfloat16),
                pltpu.VMEM((128, 128), f32),
                pltpu.VMEM((128, 128), f32),
                pltpu.VMEM((24, 128), f32),
                pltpu.VMEM((24, 128), f32),
                pltpu.VMEM((2, 4, 40, 128), f32),
                pltpu.VMEM((2, 24, 128), f32),
                pltpu.VMEM((2, 16, 128), f32),
                pltpu.VMEM((2, 16, 128), f32),
                pltpu.VMEM((2, 8, 128), f32),
                pltpu.VMEM((2, 8, 128), f32),
                pltpu.VMEM((2, 32, 1, 128), f32),
                dma((4,)), dma, dma((2, 4)), dma((2, 4)), dma((2,)), dma((2,)),
                dma((2, 4)), dma((2, 4)), dma((2, 4)), dma((2, 4)), dma((2,)), dma((2,)),
            ],
            compiler_params=pltpu.CompilerParams(collective_id=0, has_side_effects=True),
            name="pcg",
        )(jac_bus, pattern, branch_weight, bus_diag, right_side)

    axes = ("region", "blk")
    in_specs = (P("region", "blk", None, None),) + (P(axes, None),) * 4
    return jax.shard_map(
        body, mesh=mesh, in_specs=in_specs, out_specs=(P(axes, None),) * 2, check_vma=False
    )
```

```python
import jax
import jax.numpy as jnp
from jax import lax
from jax.experimental import pallas as pl
from jax.experimental.pallas import tpu as pltpu
from jax.sharding import PartitionSpec as P

ITERS = 12
MESH = pl.DeviceIdType.MESH


def farness(k):
    along_z, along_y = min(k // 8, 4 - k // 8), min(k // 2 % 4, 4 - k // 2 % 4)
    return along_z + along_y


def kernel(
    n_reg, n_blk,
    jac_hbm, pattern_ref, weight_ref, diag_ref, rhs_ref,
    sol_ref, res_ref,
    jac, jhl, jsq, pv, psm, wv, hsend, hbuf, oht, stage, picked, uv, diag, xbuf, csend, rlo16, rhi16, rlo8, rhi8, dbuf,
    jsem, psem, gsend, grecv, hsend_sem, hrecv, xsend, xrecv, rsend, rrecv, dsend, drecv,
):
    reg = lax.axis_index("region")
    blk = lax.axis_index("blk")

    def region_at(k):
        return lax.rem(reg + k + n_reg, n_reg)

    def blk_at(k):
        return lax.rem(blk + k, n_blk)

    def to_blk(k):
        return (reg, blk_at(k))

    def to_reg(k):
        return (region_at(k), blk)

    def remote(src, dst, ssem, rsem, dev):
        return pltpu.make_async_remote_copy(
            src_ref=src, dst_ref=dst, send_sem=ssem, recv_sem=rsem,
            device_id=dev, device_id_type=MESH,
        )

    jcopies = [
        pltpu.make_async_copy(jac_hbm.at[pl.ds(8 * g, 8)], jac.at[pl.ds(8 * g, 8)], jsem.at[g])
        for g in range(4)
    ]
    for c in jcopies:
        c.start()

    barrier = pltpu.get_barrier_semaphore()
    for k in range(1, n_reg):
        pl.semaphore_signal(barrier, inc=1, device_id=to_reg(k), device_id_type=MESH)
    for k in range(1, n_blk):
        pl.semaphore_signal(barrier, inc=1, device_id=to_blk(k), device_id_type=MESH)

    pv[blk] = jnp.zeros((8, 128), jnp.int32)
    pv[blk, :, 0:8] = pattern_ref[...]
    wv[blk] = weight_ref[...]
    hsend[0:8] = diag_ref[...]
    hsend[8:16] = rhs_ref[...]
    pl.semaphore_wait(barrier, n_reg - 1 + n_blk - 1)

    gcopies = []
    for k in range(1, n_blk):
        gcopies.append(remote(pv.at[blk], pv.at[blk], gsend.at[0, k], grecv.at[0, k], to_blk(k)))
        gcopies.append(remote(wv.at[blk], wv.at[blk], gsend.at[1, k], grecv.at[1, k], to_blk(k)))
    hcopies = [
        remote(hsend, hbuf.at[0], hsend_sem.at[0], hrecv.at[0], to_reg(1)),
        remote(hsend, hbuf.at[1], hsend_sem.at[1], hrecv.at[1], to_reg(-1)),
    ]
    for c in gcopies + hcopies:
        c.start()
    def halves(value):
        high = value.astype(jnp.bfloat16)
        return high, (value - high.astype(jnp.float32)).astype(jnp.bfloat16)

    def convert(t, _):
        for j in range(2):
            tile = jac[t, j]
            high, low = halves(tile)
            jhl[t, 0:128, 128 * j : 128 * j + 128] = high
            jhl[t, 128:256, 128 * j : 128 * j + 128] = low
            high, low = halves(tile * tile)
            jsq[t, 0:128, 128 * j : 128 * j + 128] = high
            jsq[t, 128:256, 128 * j : 128 * j + 128] = low
        return 0

    for c in jcopies:
        c.wait()
    lax.fori_loop(0, 32, convert, 0)

    for c in gcopies:
        c.wait_recv()
    pcopy = pltpu.make_async_copy(pv, psm, psem)
    pcopy.start()

    lane = lax.broadcasted_iota(jnp.int32, (1, 128), 1)
    patf = pv[...].astype(jnp.float32).reshape(32, 128)
    lanes32 = lax.broadcasted_iota(jnp.int32, (32, 128), 1)
    for j in range(2):
        col = jnp.sum(jnp.where(lanes32 == 2 * blk + j, patf, 0.0), axis=1, keepdims=True)
        hit = jnp.where(lanes32.astype(jnp.float32) == col, 1.0, 0.0)
        stage[32 * j : 32 * j + 32] = hit
        stage[64 + 32 * j : 96 + 32 * j] = hit
    hot = stage[...].T[0:32]
    oht[:, 0:128] = hot.astype(jnp.bfloat16)
    oht[:, 128:256] = jnp.where(lanes32 < 64, hot, 0.0).astype(jnp.bfloat16)
    weight = wv[...].reshape(32, 128)

    rows16 = lax.rem(lax.broadcasted_iota(jnp.int32, (16, 256), 0), 8)

    def group_products(lhs, mats, g, contract):
        acc = jnp.zeros((16, 256), jnp.float32)
        for k in range(8):
            out = lax.dot_general(
                lhs, mats[8 * g + k], (((1,), (contract,)), ((), ())),
                preferred_element_type=jnp.float32,
            )
            acc = jnp.where(rows16 == k, out, acc)
        return acc[8:16] + acc[0:8]

    def backward(rows, mats, par):
        parts = []
        for g in range(4):
            high, low = halves(rows[8 * g : 8 * g + 8])
            both = jnp.concatenate([high.astype(jnp.float32), low.astype(jnp.float32)], axis=0)
            lhs = jnp.concatenate([both, both], axis=1).astype(jnp.bfloat16)
            parts.append(group_products(lhs, mats, g, 0))
        whole = jnp.concatenate([p[:, 0:128] for p in parts] + [p[:, 128:256] for p in parts], axis=0)
        high = whole.astype(jnp.bfloat16)
        rest = whole - high.astype(jnp.float32)
        mid, low = halves(rest)
        stack = jnp.concatenate([high, mid, low, jnp.zeros((64, 128), jnp.bfloat16)], axis=0)
        total = jnp.dot(oht[...], stack, preferred_element_type=jnp.float32)
        csend[par] = total[0:24]

    def r_copies(par):
        return [
            remote(csend.at[par, pl.ds(16, 8)], rlo8.at[par], rsend.at[par, 0], rrecv.at[par, 0], to_reg(2)),
            remote(csend.at[par, pl.ds(0, 8)], rhi8.at[par], rsend.at[par, 1], rrecv.at[par, 1], to_reg(-2)),
            remote(csend.at[par, pl.ds(8, 16)], rlo16.at[par], rsend.at[par, 2], rrecv.at[par, 2], to_reg(1)),
            remote(csend.at[par, pl.ds(0, 16)], rhi16.at[par], rsend.at[par, 3], rrecv.at[par, 3], to_reg(-1)),
        ]

    def r_sum(par):
        before = rlo8[par] + rlo16[par, 0:8] + csend[par, 0:8]
        own = rlo16[par, 8:16] + csend[par, 8:16] + rhi16[par, 0:8]
        after = csend[par, 16:24] + rhi16[par, 8:16] + rhi8[par]
        return jnp.concatenate([before, own, after], axis=0)

    backward(weight, jsq, 0)
    copies = r_copies(0)
    for c in copies:
        c.start()
    pcopy.wait()
    for c in hcopies:
        c.wait_recv()
    for c in copies:
        c.wait_recv()
    diag[...] = jnp.concatenate([hbuf[0, 0:8], hsend[0:8], hbuf[1, 0:8]], axis=0)
    resid0 = jnp.concatenate([hbuf[0, 8:16], hsend[8:16], hbuf[1, 8:16]], axis=0)
    inv = 1.0 / (diag[...] + r_sum(0))
    for c in copies + gcopies + hcopies:
        c.wait_send()

    order = sorted(range(1, n_reg), key=farness, reverse=True)
    zeros8 = jnp.zeros((8, 128), jnp.float32)
    zeros24 = jnp.zeros((24, 128), jnp.float32)
    one = jnp.ones((1, 1), jnp.float32)

    def fold(first, second):
        both = jnp.where(lane < 64, first, second)
        rest = jnp.where(lane < 64, second, first)
        return both + pltpu.roll(rest, 64, 1)

    def step(i, carry):
        solution, direction, resid, along, gamma_old, alpha_old = carry
        par = lax.rem(i, 2)
        rpar = lax.rem(i + 1, 2)
        scaled = inv * resid
        uv[...] = scaled
        own_u = scaled[8:16]
        first = jnp.sum(own_u * resid[8:16], axis=0, keepdims=True)
        second = jnp.sum(own_u * own_u * diag[8:16], axis=0, keepdims=True)
        xbuf[par, blk, 32:33] = fold(first, second)

        for t in range(32):
            for j in range(2):
                source = pl.ds(psm[t // 8, t % 8, 2 * blk + j], 1)
                picked[t : t + 1, 128 * j : 128 * j + 128] = uv[source, :]
        for g in range(4):
            value = picked[8 * g : 8 * g + 8]
            high = value.astype(jnp.bfloat16).astype(jnp.float32)
            lhs = jnp.concatenate([high, value - high], axis=0).astype(jnp.bfloat16)
            out = group_products(lhs, jhl, g, 1)
            xbuf[par, blk, 8 * g : 8 * g + 8] = out[:, 0:128] + out[:, 128:256]
        xcopies = [
            remote(xbuf.at[par, blk, pl.ds(0, 33)], xbuf.at[par, blk, pl.ds(0, 33)], xsend.at[par, k], xrecv.at[par, k], to_blk(k))
            for k in (2, 1, 3)
        ]
        for c in xcopies:
            c.start()
        for c in xcopies:
            c.wait_recv()
        rows = xbuf[par, 0, 0:32] + xbuf[par, 1, 0:32] + xbuf[par, 2, 0:32] + xbuf[par, 3, 0:32]
        scal = xbuf[par, 0, 32:33] + xbuf[par, 1, 32:33] + xbuf[par, 2, 32:33] + xbuf[par, 3, 32:33]
        weighted = weight * rows
        energy = jnp.sum(weighted * rows, axis=0, keepdims=True)
        dbuf[par, reg] = scal + fold(jnp.zeros((1, 128), jnp.float32), energy)
        dcopies = [
            remote(dbuf.at[par, reg], dbuf.at[par, reg], dsend.at[par], drecv.at[par], to_reg(k))
            for k in order
        ]
        for c in dcopies:
            c.start()
        backward(weighted, jhl, rpar)
        rcopies = r_copies(rpar)
        for c in rcopies:
            c.start()
        for c in rcopies:
            c.wait_recv()
        image = diag[...] * scaled + r_sum(rpar)
        others = dbuf.at[par, pl.ds(0, n_reg - 1)]
        dall = remote(others, others, dsend.at[par], drecv.at[par], to_reg(1))
        dall.wait_recv()
        sums = jnp.sum(dbuf[par].reshape(n_reg, 128), axis=0, keepdims=True)
        gamma = jnp.sum(jnp.where(lane < 64, sums, 0.0), axis=1, keepdims=True)
        delta = jnp.sum(jnp.where(lane < 64, 0.0, sums), axis=1, keepdims=True)
        begun = jnp.where(i == 0, 0.0, 1.0)
        beta = begun * gamma / gamma_old
        alpha = gamma / (delta - beta * gamma / alpha_old)
        direction = own_u + beta * direction
        along = image + beta * along
        solution = solution + alpha * direction
        resid = resid - alpha * along
        for c in xcopies + rcopies + [dall]:
            c.wait_send()
        return (solution, direction, resid, along, gamma, alpha)

    carry = lax.fori_loop(0, ITERS, step, (zeros8, zeros8, resid0, zeros24, one, one))
    sol_ref[...] = carry[0]
    res_ref[...] = carry[2][8:16]


def solution(mesh):
    n_reg, n_blk = mesh.shape["region"], mesh.shape["blk"]
    f32 = jnp.float32

    def body(jac_bus, pattern, branch_weight, bus_diag, right_side):
        vmem = pl.BlockSpec(memory_space=pltpu.VMEM)
        shape = jax.ShapeDtypeStruct((8, 128), f32)
        dma = pltpu.SemaphoreType.DMA

        def call(*args):
            return kernel(n_reg, n_blk, *args)

        return pl.pallas_call(
            call,
            out_shape=(shape, shape),
            in_specs=[pl.BlockSpec(memory_space=pl.ANY)] + [vmem] * 4,
            out_specs=(vmem, vmem),
            scratch_shapes=[
                pltpu.VMEM((32, 2, 128, 128), f32),
                pltpu.VMEM((32, 256, 256), jnp.bfloat16),
                pltpu.VMEM((32, 256, 256), jnp.bfloat16),
                pltpu.VMEM((4, 8, 128), jnp.int32),
                pltpu.SMEM((4, 8, 128), jnp.int32),
                pltpu.VMEM((4, 8, 128), f32),
                pltpu.VMEM((16, 128), f32),
                pltpu.VMEM((2, 16, 128), f32),
                pltpu.VMEM((32, 256), jnp.bfloat16),
                pltpu.VMEM((128, 128), f32),
                pltpu.VMEM((32, 256), f32),
                pltpu.VMEM((24, 128), f32),
                pltpu.VMEM((24, 128), f32),
                pltpu.VMEM((2, 4, 40, 128), f32),
                pltpu.VMEM((2, 24, 128), f32),
                pltpu.VMEM((2, 16, 128), f32),
                pltpu.VMEM((2, 16, 128), f32),
                pltpu.VMEM((2, 8, 128), f32),
                pltpu.VMEM((2, 8, 128), f32),
                pltpu.VMEM((2, 32, 1, 128), f32),
                dma((4,)), dma, dma((2, 4)), dma((2, 4)), dma((2,)), dma((2,)),
                dma((2, 4)), dma((2, 4)), dma((2, 4)), dma((2, 4)), dma((2,)), dma((2,)),
            ],
            compiler_params=pltpu.CompilerParams(collective_id=0, has_side_effects=True),
            name="pcg",
        )(jac_bus, pattern, branch_weight, bus_diag, right_side)

    axes = ("region", "blk")
    in_specs = (P("region", "blk", None, None),) + (P(axes, None),) * 4
    return jax.shard_map(
        body, mesh=mesh, in_specs=in_specs, out_specs=(P(axes, None),) * 2, check_vma=False
    )
```

```python
import jax
import jax.numpy as jnp
from jax import lax
from jax.experimental import pallas as pl
from jax.experimental.pallas import tpu as pltpu
from jax.sharding import PartitionSpec as P

ITERS = 12
MESH = pl.DeviceIdType.MESH


def farness(k):
    along_z, along_y = min(k // 8, 4 - k // 8), min(k // 2 % 4, 4 - k // 2 % 4)
    return along_z + along_y


def kernel(
    n_reg, n_blk,
    jac_hbm, pattern_ref, weight_ref, diag_ref, rhs_ref,
    sol_ref, res_ref,
    jac, pv, psm, wv, hsend, hbuf, oht, stage, part, uv, diag, xbuf, csend, rlo16, rhi16, rlo8, rhi8, dbuf,
    jsem, psem, gsend, grecv, hsend_sem, hrecv, xsend, xrecv, rsend, rrecv, dsend, drecv,
):
    reg = lax.axis_index("region")
    blk = lax.axis_index("blk")

    def region_at(k):
        return lax.rem(reg + k + n_reg, n_reg)

    def blk_at(k):
        return lax.rem(blk + k, n_blk)

    def to_blk(k):
        return (reg, blk_at(k))

    def to_reg(k):
        return (region_at(k), blk)

    def remote(src, dst, ssem, rsem, dev):
        return pltpu.make_async_remote_copy(
            src_ref=src, dst_ref=dst, send_sem=ssem, recv_sem=rsem,
            device_id=dev, device_id_type=MESH,
        )

    jcopies = [
        pltpu.make_async_copy(jac_hbm.at[pl.ds(8 * g, 8)], jac.at[pl.ds(8 * g, 8)], jsem.at[g])
        for g in range(4)
    ]
    for c in jcopies:
        c.start()

    barrier = pltpu.get_barrier_semaphore()
    for k in range(1, n_reg):
        pl.semaphore_signal(barrier, inc=1, device_id=to_reg(k), device_id_type=MESH)
    for k in range(1, n_blk):
        pl.semaphore_signal(barrier, inc=1, device_id=to_blk(k), device_id_type=MESH)

    pv[blk] = jnp.zeros((8, 128), jnp.int32)
    pv[blk, :, 0:8] = pattern_ref[...]
    wv[blk] = weight_ref[...]
    hsend[0:8] = diag_ref[...]
    hsend[8:16] = rhs_ref[...]
    pl.semaphore_wait(barrier, n_reg - 1 + n_blk - 1)

    gcopies = []
    for k in range(1, n_blk):
        gcopies.append(remote(pv.at[blk], pv.at[blk], gsend.at[0, k], grecv.at[0, k], to_blk(k)))
        gcopies.append(remote(wv.at[blk], wv.at[blk], gsend.at[1, k], grecv.at[1, k], to_blk(k)))
    hcopies = [
        remote(hsend, hbuf.at[0], hsend_sem.at[0], hrecv.at[0], to_reg(1)),
        remote(hsend, hbuf.at[1], hsend_sem.at[1], hrecv.at[1], to_reg(-1)),
    ]
    for c in gcopies + hcopies:
        c.start()
    for c in gcopies:
        c.wait_recv()
    pcopy = pltpu.make_async_copy(pv, psm, psem)
    pcopy.start()

    lane = lax.broadcasted_iota(jnp.int32, (1, 128), 1)
    patf = pv[...].astype(jnp.float32).reshape(32, 128)
    lanes32 = lax.broadcasted_iota(jnp.int32, (32, 128), 1)
    for j in range(2):
        col = jnp.sum(jnp.where(lanes32 == 2 * blk + j, patf, 0.0), axis=1, keepdims=True)
        hit = jnp.where(lanes32.astype(jnp.float32) == col, 1.0, 0.0)
        stage[32 * j : 32 * j + 32] = hit
        stage[64 + 32 * j : 96 + 32 * j] = hit
    hot = stage[...].T[0:32]
    oht[:, 0:128] = hot.astype(jnp.bfloat16)
    oht[:, 128:256] = jnp.where(lanes32 < 64, hot, 0.0).astype(jnp.bfloat16)
    weight = wv[...].reshape(32, 128)

    def eight_sums(terms):
        total = terms[0:8]
        for k in range(1, 16):
            total = total + terms[8 * k : 8 * k + 8]
        return total

    def group_rows(slot):
        total = part[slot, pl.ds(0, 8, stride=8), :]
        for k in range(1, 8):
            total = total + part[slot, pl.ds(k, 8, stride=8), :]
        return total

    def backward(rows, square, par):
        for t in range(32):
            wc = jnp.broadcast_to(rows[t : t + 1], (128, 128)).T
            for j in range(2):
                tile = jac[t, j]
                term = tile * wc
                if square:
                    term = term * tile
                part[4 * j + t // 8, 8 * (t % 8) : 8 * (t % 8) + 8] = eight_sums(term)
        whole = jnp.concatenate([group_rows(k) for k in range(8)], axis=0)
        high = whole.astype(jnp.bfloat16)
        rest = whole - high.astype(jnp.float32)
        mid = rest.astype(jnp.bfloat16)
        low = (rest - mid.astype(jnp.float32)).astype(jnp.bfloat16)
        stack = jnp.concatenate([high, mid, low, jnp.zeros((64, 128), jnp.bfloat16)], axis=0)
        total = jnp.dot(oht[...], stack, preferred_element_type=jnp.float32)
        csend[par] = total[0:24]

    def r_copies(par):
        return [
            remote(csend.at[par, pl.ds(16, 8)], rlo8.at[par], rsend.at[par, 0], rrecv.at[par, 0], to_reg(2)),
            remote(csend.at[par, pl.ds(0, 8)], rhi8.at[par], rsend.at[par, 1], rrecv.at[par, 1], to_reg(-2)),
            remote(csend.at[par, pl.ds(8, 16)], rlo16.at[par], rsend.at[par, 2], rrecv.at[par, 2], to_reg(1)),
            remote(csend.at[par, pl.ds(0, 16)], rhi16.at[par], rsend.at[par, 3], rrecv.at[par, 3], to_reg(-1)),
        ]

    def r_sum(par):
        before = rlo8[par] + rlo16[par, 0:8] + csend[par, 0:8]
        own = rlo16[par, 8:16] + csend[par, 8:16] + rhi16[par, 0:8]
        after = csend[par, 16:24] + rhi16[par, 8:16] + rhi8[par]
        return jnp.concatenate([before, own, after], axis=0)

    for c in jcopies:
        c.wait()
    backward(weight, True, 0)
    copies = r_copies(0)
    for c in copies:
        c.start()
    pcopy.wait()
    for c in hcopies:
        c.wait_recv()
    for c in copies:
        c.wait_recv()
    diag[...] = jnp.concatenate([hbuf[0, 0:8], hsend[0:8], hbuf[1, 0:8]], axis=0)
    resid0 = jnp.concatenate([hbuf[0, 8:16], hsend[8:16], hbuf[1, 8:16]], axis=0)
    inv = 1.0 / (diag[...] + r_sum(0))
    for c in copies + gcopies + hcopies:
        c.wait_send()

    order = sorted(range(1, n_reg), key=farness, reverse=True)
    zeros8 = jnp.zeros((8, 128), jnp.float32)
    zeros24 = jnp.zeros((24, 128), jnp.float32)
    one = jnp.ones((1, 1), jnp.float32)

    def fold(first, second):
        both = jnp.where(lane < 64, first, second)
        rest = jnp.where(lane < 64, second, first)
        return both + pltpu.roll(rest, 64, 1)

    def step(i, carry):
        solution, direction, resid, along, gamma_old, alpha_old = carry
        par = lax.rem(i, 2)
        rpar = lax.rem(i + 1, 2)
        scaled = inv * resid
        uv[...] = scaled
        own_u = scaled[8:16]
        first = jnp.sum(own_u * resid[8:16], axis=0, keepdims=True)
        second = jnp.sum(own_u * own_u * diag[8:16], axis=0, keepdims=True)
        xbuf[par, blk, 32:33] = fold(first, second)

        for t in range(32):
            x0 = uv[pl.ds(psm[t // 8, t % 8, 2 * blk], 1), :]
            x1 = uv[pl.ds(psm[t // 8, t % 8, 2 * blk + 1], 1), :]
            both = jac[t, 0] * x0 + jac[t, 1] * x1
            part[t // 8, 8 * (t % 8) : 8 * (t % 8) + 8] = eight_sums(both.T)
        for g in range(4):
            xbuf[par, blk, 8 * g : 8 * g + 8] = group_rows(g)
        xcopies = [
            remote(xbuf.at[par, blk, pl.ds(0, 33)], xbuf.at[par, blk, pl.ds(0, 33)], xsend.at[par, k], xrecv.at[par, k], to_blk(k))
            for k in (2, 1, 3)
        ]
        for c in xcopies:
            c.start()
        for c in xcopies:
            c.wait_recv()
        rows = xbuf[par, 0, 0:32] + xbuf[par, 1, 0:32] + xbuf[par, 2, 0:32] + xbuf[par, 3, 0:32]
        scal = xbuf[par, 0, 32:33] + xbuf[par, 1, 32:33] + xbuf[par, 2, 32:33] + xbuf[par, 3, 32:33]
        weighted = weight * rows
        energy = jnp.sum(weighted * rows, axis=0, keepdims=True)
        dbuf[par, reg] = scal + fold(jnp.zeros((1, 128), jnp.float32), energy)
        dcopies = [
            remote(dbuf.at[par, reg], dbuf.at[par, reg], dsend.at[par], drecv.at[par], to_reg(k))
            for k in order
        ]
        for c in dcopies:
            c.start()
        backward(weighted, False, rpar)
        rcopies = r_copies(rpar)
        for c in rcopies:
            c.start()
        for c in rcopies:
            c.wait_recv()
        image = diag[...] * scaled + r_sum(rpar)
        others = dbuf.at[par, pl.ds(0, n_reg - 1)]
        dall = remote(others, others, dsend.at[par], drecv.at[par], to_reg(1))
        dall.wait_recv()
        sums = jnp.sum(dbuf[par].reshape(n_reg, 128), axis=0, keepdims=True)
        gamma = jnp.sum(jnp.where(lane < 64, sums, 0.0), axis=1, keepdims=True)
        delta = jnp.sum(jnp.where(lane < 64, 0.0, sums), axis=1, keepdims=True)
        begun = jnp.where(i == 0, 0.0, 1.0)
        beta = begun * gamma / gamma_old
        alpha = gamma / (delta - beta * gamma / alpha_old)
        direction = own_u + beta * direction
        along = image + beta * along
        solution = solution + alpha * direction
        resid = resid - alpha * along
        for c in xcopies + rcopies + [dall]:
            c.wait_send()
        return (solution, direction, resid, along, gamma, alpha)

    carry = lax.fori_loop(0, ITERS, step, (zeros8, zeros8, resid0, zeros24, one, one))
    sol_ref[...] = carry[0]
    res_ref[...] = carry[2][8:16]


def solution(mesh):
    n_reg, n_blk = mesh.shape["region"], mesh.shape["blk"]
    f32 = jnp.float32

    def body(jac_bus, pattern, branch_weight, bus_diag, right_side):
        vmem = pl.BlockSpec(memory_space=pltpu.VMEM)
        shape = jax.ShapeDtypeStruct((8, 128), f32)
        dma = pltpu.SemaphoreType.DMA

        def call(*args):
            return kernel(n_reg, n_blk, *args)

        return pl.pallas_call(
            call,
            out_shape=(shape, shape),
            in_specs=[pl.BlockSpec(memory_space=pl.ANY)] + [vmem] * 4,
            out_specs=(vmem, vmem),
            scratch_shapes=[
                pltpu.VMEM((32, 2, 128, 128), f32),
                pltpu.VMEM((4, 8, 128), jnp.int32),
                pltpu.SMEM((4, 8, 128), jnp.int32),
                pltpu.VMEM((4, 8, 128), f32),
                pltpu.VMEM((16, 128), f32),
                pltpu.VMEM((2, 16, 128), f32),
                pltpu.VMEM((32, 256), jnp.bfloat16),
                pltpu.VMEM((128, 128), f32),
                pltpu.VMEM((8, 64, 128), f32),
                pltpu.VMEM((24, 128), f32),
                pltpu.VMEM((24, 128), f32),
                pltpu.VMEM((2, 4, 40, 128), f32),
                pltpu.VMEM((2, 24, 128), f32),
                pltpu.VMEM((2, 16, 128), f32),
                pltpu.VMEM((2, 16, 128), f32),
                pltpu.VMEM((2, 8, 128), f32),
                pltpu.VMEM((2, 8, 128), f32),
                pltpu.VMEM((2, 32, 1, 128), f32),
                dma((4,)), dma, dma((2, 4)), dma((2, 4)), dma((2,)), dma((2,)),
                dma((2, 4)), dma((2, 4)), dma((2, 4)), dma((2, 4)), dma((2,)), dma((2,)),
            ],
            compiler_params=pltpu.CompilerParams(collective_id=0, has_side_effects=True),
            name="pcg",
        )(jac_bus, pattern, branch_weight, bus_diag, right_side)

    axes = ("region", "blk")
    in_specs = (P("region", "blk", None, None),) + (P(axes, None),) * 4
    return jax.shard_map(
        body, mesh=mesh, in_specs=in_specs, out_specs=(P(axes, None),) * 2, check_vma=False
    )
```

```python
import jax
import jax.numpy as jnp
from jax import lax
from jax.experimental import pallas as pl
from jax.experimental.pallas import tpu as pltpu
from jax.sharding import PartitionSpec as P

ITERS = 12
CHUNKS = 2
SPAN = 32 // CHUNKS
MESH = pl.DeviceIdType.MESH


def farness(k):
    along_z, along_y = min(k // 8, 4 - k // 8), min(k // 2 % 4, 4 - k // 2 % 4)
    return along_z + along_y


def kernel(
    n_reg, n_blk,
    jac_hbm, pattern_hbm, weight_hbm, diag_hbm, rhs_hbm,
    out_ref,
    jac, pat, pv, psm, wv, hsend, hbuf, oht, stage, part, uv, diag, xbuf, csend, rlo16, rhi16, rlo8, rhi8, dbuf,
    jsem, isem, far_sem, psem, gsend, grecv, hsend_sem, hrecv, xsend, xrecv, rsend, rrecv, dsend, drecv,
):
    reg = lax.axis_index("region")
    blk = lax.axis_index("blk")

    def region_at(k):
        return lax.rem(reg + k + n_reg, n_reg)

    def blk_at(k):
        return lax.rem(blk + k, n_blk)

    def to_blk(k):
        return (reg, blk_at(k))

    def to_reg(k):
        return (region_at(k), blk)

    def remote(src, dst, ssem, rsem, dev):
        return pltpu.make_async_remote_copy(
            src_ref=src, dst_ref=dst, send_sem=ssem, recv_sem=rsem,
            device_id=dev, device_id_type=MESH,
        )

    jcopies = [
        pltpu.make_async_copy(jac_hbm.at[pl.ds(8 * g, 8)], jac.at[pl.ds(8 * g, 8)], jsem.at[g])
        for g in range(4)
    ]
    icopies = [
        pltpu.make_async_copy(pattern_hbm, pat, isem.at[0]),
        pltpu.make_async_copy(weight_hbm, wv.at[blk], isem.at[1]),
        pltpu.make_async_copy(diag_hbm, hsend.at[pl.ds(0, 8)], isem.at[2]),
        pltpu.make_async_copy(rhs_hbm, hsend.at[pl.ds(8, 8)], isem.at[3]),
    ]
    for c in icopies + jcopies:
        c.start()

    barrier = pltpu.get_barrier_semaphore()
    near = [to_blk(k) for k in range(1, n_blk)] + [to_reg(k) for k in (1, -1, 2, -2)]
    for dev in near:
        pl.semaphore_signal(barrier, inc=1, device_id=dev, device_id_type=MESH)

    def far_signal(n):
        for k in (2 << n, -(2 << n)):
            pl.semaphore_signal(far_sem.at[n], inc=1, device_id=to_reg(k), device_id_type=MESH)

    pv[blk] = jnp.zeros((8, 128), jnp.int32)
    for c in icopies:
        c.wait()
    pv[blk, :, 0:8] = pat[...]
    pl.semaphore_wait(barrier, len(near))

    gcopies = []
    for k in range(1, n_blk):
        gcopies.append(remote(pv.at[blk], pv.at[blk], gsend.at[0, k], grecv.at[0, k], to_blk(k)))
        gcopies.append(remote(wv.at[blk], wv.at[blk], gsend.at[1, k], grecv.at[1, k], to_blk(k)))
    hcopies = [
        remote(hsend, hbuf.at[0], hsend_sem.at[0], hrecv.at[0], to_reg(1)),
        remote(hsend, hbuf.at[1], hsend_sem.at[1], hrecv.at[1], to_reg(-1)),
    ]
    for c in gcopies + hcopies:
        c.start()
    far_signal(0)
    pl.semaphore_wait(far_sem.at[0], 2)
    far_signal(1)
    for c in gcopies:
        c.wait_recv()
    pcopy = pltpu.make_async_copy(pv, psm, psem)
    pcopy.start()

    lane = lax.broadcasted_iota(jnp.int32, (1, 128), 1)
    patf = pv[...].astype(jnp.float32).reshape(32, 128)
    lanes32 = lax.broadcasted_iota(jnp.int32, (32, 128), 1)
    for j in range(2):
        col = jnp.sum(jnp.where(lanes32 == 2 * blk + j, patf, 0.0), axis=1, keepdims=True)
        hit = jnp.where(lanes32.astype(jnp.float32) == col, 1.0, 0.0)
        stage[32 * j : 32 * j + 32] = hit
        stage[64 + 32 * j : 96 + 32 * j] = hit
    hot = stage[...].T[0:32]
    oht[:, 0:128] = hot.astype(jnp.bfloat16)
    oht[:, 128:256] = jnp.where(lanes32 < 64, hot, 0.0).astype(jnp.bfloat16)
    weight = wv[...].reshape(32, 128)

    def eight_sums(terms):
        total = terms[0:8]
        for k in range(1, 16):
            total = total + terms[8 * k : 8 * k + 8]
        return total

    def group_rows(slot):
        total = part[slot, pl.ds(0, 8, stride=8), :]
        for k in range(1, 8):
            total = total + part[slot, pl.ds(k, 8, stride=8), :]
        return total

    def backward_tiles(first, rows, square):
        for t in range(first, first + rows.shape[0]):
            wc = jnp.broadcast_to(rows[t - first : t - first + 1], (128, 128)).T
            for j in range(2):
                tile = jac[t, j]
                term = tile * wc
                if square:
                    term = term * tile
                part[4 * j + t // 8, 8 * (t % 8) : 8 * (t % 8) + 8] = eight_sums(term)

    def backward_end(par):
        whole = jnp.concatenate([group_rows(k) for k in range(8)], axis=0)
        high = whole.astype(jnp.bfloat16)
        rest = whole - high.astype(jnp.float32)
        mid = rest.astype(jnp.bfloat16)
        low = (rest - mid.astype(jnp.float32)).astype(jnp.bfloat16)
        stack = jnp.concatenate([high, mid, low, jnp.zeros((64, 128), jnp.bfloat16)], axis=0)
        total = jnp.dot(oht[...], stack, preferred_element_type=jnp.float32)
        csend[par] = total[0:24]

    def r_copies(par):
        return [
            remote(csend.at[par, pl.ds(16, 8)], rlo8.at[par], rsend.at[par, 0], rrecv.at[par, 0], to_reg(2)),
            remote(csend.at[par, pl.ds(0, 8)], rhi8.at[par], rsend.at[par, 1], rrecv.at[par, 1], to_reg(-2)),
            remote(csend.at[par, pl.ds(8, 16)], rlo16.at[par], rsend.at[par, 2], rrecv.at[par, 2], to_reg(1)),
            remote(csend.at[par, pl.ds(0, 16)], rhi16.at[par], rsend.at[par, 3], rrecv.at[par, 3], to_reg(-1)),
        ]

    def r_sum(par):
        before = rlo8[par] + rlo16[par, 0:8] + csend[par, 0:8]
        own = rlo16[par, 8:16] + csend[par, 8:16] + rhi16[par, 0:8]
        after = csend[par, 16:24] + rhi16[par, 8:16] + rhi8[par]
        return jnp.concatenate([before, own, after], axis=0)

    for c in jcopies:
        c.wait()
    backward_tiles(0, weight, True)
    backward_end(0)
    copies = r_copies(0)
    for c in copies:
        c.start()
    pl.semaphore_wait(far_sem.at[1], 2)
    far_signal(2)
    pcopy.wait()
    for c in hcopies:
        c.wait_recv()
    for c in copies:
        c.wait_recv()
    diag[...] = jnp.concatenate([hbuf[0, 0:8], hsend[0:8], hbuf[1, 0:8]], axis=0)
    resid0 = jnp.concatenate([hbuf[0, 8:16], hsend[8:16], hbuf[1, 8:16]], axis=0)
    inv = 1.0 / (diag[...] + r_sum(0))
    for c in copies + gcopies + hcopies:
        c.wait_send()
    pl.semaphore_wait(far_sem.at[2], 2)

    order = sorted(range(1, n_reg), key=farness, reverse=True)
    zeros8 = jnp.zeros((8, 128), jnp.float32)
    zeros24 = jnp.zeros((24, 128), jnp.float32)
    one = jnp.ones((1, 1), jnp.float32)

    def fold(first, second):
        both = jnp.where(lane < 64, first, second)
        rest = jnp.where(lane < 64, second, first)
        return both + pltpu.roll(rest, 64, 1)

    def step(i, carry):
        solution, direction, resid, along, gamma_old, alpha_old = carry
        par = lax.rem(i, 2)
        rpar = lax.rem(i + 1, 2)
        scaled = inv * resid
        uv[...] = scaled
        own_u = scaled[8:16]
        first = jnp.sum(own_u * resid[8:16], axis=0, keepdims=True)
        second = jnp.sum(own_u * own_u * diag[8:16], axis=0, keepdims=True)
        xbuf[par, blk, SPAN : SPAN + 1] = fold(first, second)

        xcopies = []
        for c in range(CHUNKS):
            for t in range(SPAN * c, SPAN * c + SPAN):
                x0 = uv[pl.ds(psm[t // 8, t % 8, 2 * blk], 1), :]
                x1 = uv[pl.ds(psm[t // 8, t % 8, 2 * blk + 1], 1), :]
                both = jac[t, 0] * x0 + jac[t, 1] * x1
                part[t // 8, 8 * (t % 8) : 8 * (t % 8) + 8] = eight_sums(both.T)
            at = SPAN * c + (8 if c else 0)
            for g in range(SPAN // 8):
                xbuf[par, blk, at + 8 * g : at + 8 * g + 8] = group_rows(SPAN // 8 * c + g)
            mine = xbuf.at[par, blk, pl.ds(at, SPAN if c else SPAN + 1)]
            xcopies.append([
                remote(mine, mine, xsend.at[par, c, k], xrecv.at[par, c, k], to_blk(k))
                for k in (2, 1, 3)
            ])
            for copy in xcopies[c]:
                copy.start()
        energy = jnp.zeros((1, 128), jnp.float32)
        for c in range(CHUNKS):
            for copy in xcopies[c]:
                copy.wait_recv()
            at = SPAN * c + (8 if c else 0)
            b0, b1, b2, b3 = (xbuf[par, b, at : at + SPAN] for b in range(4))
            rows = b0 + b1 + b2 + b3
            weighted = weight[SPAN * c : SPAN * c + SPAN] * rows
            energy = energy + jnp.sum(weighted * rows, axis=0, keepdims=True)
            if c < CHUNKS - 1:
                backward_tiles(SPAN * c, weighted, False)
        b0, b1, b2, b3 = (xbuf[par, b, SPAN : SPAN + 1] for b in range(4))
        dbuf[par, reg] = b0 + b1 + b2 + b3 + fold(jnp.zeros((1, 128), jnp.float32), energy)
        dcopies = [
            remote(dbuf.at[par, reg], dbuf.at[par, reg], dsend.at[par], drecv.at[par], to_reg(k))
            for k in order
        ]
        for c in dcopies:
            c.start()
        backward_tiles(32 - SPAN, weighted, False)
        backward_end(rpar)
        rcopies = r_copies(rpar)
        for c in rcopies:
            c.start()
        for c in rcopies:
            c.wait_recv()
        image = diag[...] * scaled + r_sum(rpar)
        others = dbuf.at[par, pl.ds(0, n_reg - 1)]
        dall = remote(others, others, dsend.at[par], drecv.at[par], to_reg(1))
        dall.wait_recv()
        sums = jnp.sum(dbuf[par].reshape(n_reg, 128), axis=0, keepdims=True)
        gamma = jnp.sum(jnp.where(lane < 64, sums, 0.0), axis=1, keepdims=True)
        delta = jnp.sum(jnp.where(lane < 64, 0.0, sums), axis=1, keepdims=True)
        begun = jnp.where(i == 0, 0.0, 1.0)
        beta = begun * gamma / gamma_old
        alpha = gamma / (delta - beta * gamma / alpha_old)
        direction = own_u + beta * direction
        along = image + beta * along
        out_ref[0:8] = solution
        out_ref[8:16] = direction
        out_ref[16:24] = resid[8:16]
        out_ref[24:32] = along[8:16]
        out_ref[32:40] = jnp.broadcast_to(alpha, (8, 128))
        solution = solution + alpha * direction
        resid = resid - alpha * along
        for c in sum(xcopies, []) + rcopies + [dall]:
            c.wait_send()
        return (solution, direction, resid, along, gamma, alpha)

    lax.fori_loop(0, ITERS, step, (zeros8, zeros8, resid0, zeros24, one, one))


def solution(mesh):
    n_reg, n_blk = mesh.shape["region"], mesh.shape["blk"]
    f32 = jnp.float32

    def body(jac_bus, pattern, branch_weight, bus_diag, right_side):
        vmem = pl.BlockSpec(memory_space=pltpu.VMEM)
        shape = jax.ShapeDtypeStruct((40, 128), f32)
        dma = pltpu.SemaphoreType.DMA

        def call(*args):
            return kernel(n_reg, n_blk, *args)

        last = pl.pallas_call(
            call,
            out_shape=shape,
            in_specs=[pl.BlockSpec(memory_space=pl.ANY)] * 5,
            out_specs=vmem,
            scratch_shapes=[
                pltpu.VMEM((32, 2, 128, 128), f32),
                pltpu.VMEM((8, 8), jnp.int32),
                pltpu.VMEM((4, 8, 128), jnp.int32),
                pltpu.SMEM((4, 8, 128), jnp.int32),
                pltpu.VMEM((4, 8, 128), f32),
                pltpu.VMEM((16, 128), f32),
                pltpu.VMEM((2, 16, 128), f32),
                pltpu.VMEM((32, 256), jnp.bfloat16),
                pltpu.VMEM((128, 128), f32),
                pltpu.VMEM((8, 64, 128), f32),
                pltpu.VMEM((24, 128), f32),
                pltpu.VMEM((24, 128), f32),
                pltpu.VMEM((2, 4, 40, 128), f32),
                pltpu.VMEM((2, 24, 128), f32),
                pltpu.VMEM((2, 16, 128), f32),
                pltpu.VMEM((2, 16, 128), f32),
                pltpu.VMEM((2, 8, 128), f32),
                pltpu.VMEM((2, 8, 128), f32),
                pltpu.VMEM((2, 32, 1, 128), f32),
                dma((4,)), dma((4,)), pltpu.SemaphoreType.REGULAR((3,)), dma, dma((2, 4)), dma((2, 4)), dma((2,)), dma((2,)),
                dma((2, CHUNKS, 4)), dma((2, CHUNKS, 4)), dma((2, 4)), dma((2, 4)), dma((2,)), dma((2,)),
            ],
            compiler_params=pltpu.CompilerParams(collective_id=0, has_side_effects=True),
            name="pcg",
        )(jac_bus, pattern, branch_weight, bus_diag, right_side)
        before, direction, resid, along, alpha = (last[8 * k : 8 * k + 8] for k in range(5))
        return before + alpha * direction, resid - alpha * along

    axes = ("region", "blk")
    in_specs = (P("region", "blk", None, None),) + (P(axes, None),) * 4
    return jax.shard_map(
        body, mesh=mesh, in_specs=in_specs, out_specs=(P(axes, None),) * 2, check_vma=False
    )
```

```python
import jax
import jax.numpy as jnp
from jax import lax
from jax.experimental import pallas as pl
from jax.experimental.pallas import tpu as pltpu
from jax.sharding import PartitionSpec as P

ITERS = 12
EARLY = 18
EACH = 18
INTO = 6
CHUNKS = 2
SPAN = 32 // CHUNKS
MESH = pl.DeviceIdType.MESH


def farness(offset):
    steps = [min(n, 4 - n) for n in offset[:2]]
    return (min(steps) > 0, sum(steps), offset[2] == 0)


def kernel(
    n_reg, n_blk,
    jac_hbm, pattern_hbm, weight_hbm, diag_hbm, rhs_hbm,
    out_ref,
    jac, pat, pv, psm, wv, hsend, hbuf, oht, stage, part, uv, diag, xbuf, csend, rlo16, rhi16, rlo8, rhi8, dbuf,
    jsem, isem, far_sem, psem, gsend, grecv, hsend_sem, hrecv, xsend, xrecv, rsend, rrecv, dsend, drecv,
):
    reg = lax.axis_index("region")
    blk = lax.axis_index("blk")

    def region_at(k):
        return lax.rem(reg + k + n_reg, n_reg)

    def blk_at(k):
        return lax.rem(blk + k, n_blk)

    def to_blk(k):
        return (reg, blk_at(k))

    def to_reg(k):
        return (region_at(k), blk)

    def remote(src, dst, ssem, rsem, dev):
        return pltpu.make_async_remote_copy(
            src_ref=src, dst_ref=dst, send_sem=ssem, recv_sem=rsem,
            device_id=dev, device_id_type=MESH,
        )

    jcopies = [
        pltpu.make_async_copy(jac_hbm, jac, jsem)
        for _ in range(1)
    ]
    icopies = [
        pltpu.make_async_copy(pattern_hbm, pat, isem.at[1]),
        pltpu.make_async_copy(weight_hbm, wv.at[blk], isem.at[0]),
        pltpu.make_async_copy(diag_hbm, hsend.at[pl.ds(0, 8)], isem.at[0]),
        pltpu.make_async_copy(rhs_hbm, hsend.at[pl.ds(8, 8)], isem.at[0]),
    ]
    for c in icopies + jcopies:
        c.start()

    barrier = pltpu.get_barrier_semaphore()
    near = [to_blk(k) for k in range(1, n_blk)] + [to_reg(k) for k in (1, -1, 2, -2)]
    for dev in near:
        pl.semaphore_signal(barrier, inc=1, device_id=dev, device_id_type=MESH)

    def far_signal(n):
        for k in (2 << n, -(2 << n)):
            pl.semaphore_signal(far_sem.at[n], inc=1, device_id=to_reg(k), device_id_type=MESH)

    pv[blk] = jnp.zeros((8, 128), jnp.int32)
    icopies[0].wait()
    landed = stage.at[pl.ds(0, 24)]
    pltpu.make_async_copy(landed, landed, isem.at[0]).wait()
    pv[blk, :, 0:8] = pat[...]
    pl.semaphore_wait(barrier, len(near))

    gcopies = []
    for k in range(1, n_blk):
        gcopies.append(remote(pv.at[blk], pv.at[blk], gsend.at[0], grecv.at[0], to_blk(k)))
        gcopies.append(remote(wv.at[blk], wv.at[blk], gsend.at[1], grecv.at[1], to_blk(k)))
    hcopies = [
        remote(hsend, hbuf.at[0], hsend_sem, hrecv, to_reg(1)),
        remote(hsend, hbuf.at[1], hsend_sem, hrecv, to_reg(-1)),
    ]
    for c in gcopies + hcopies:
        c.start()

    def whole(ref, ssem, rsem):
        return remote(ref, ref, ssem, rsem, to_blk(1))

    gcopies = [
        whole(pv.at[pl.ds(0, n_blk - 1)], gsend.at[0], grecv.at[0]),
        whole(wv.at[pl.ds(0, n_blk - 1)], gsend.at[1], grecv.at[1]),
    ]
    hcopies = [whole(hbuf, hsend_sem, hrecv)]
    far_signal(0)
    pl.semaphore_wait(far_sem.at[0], 2)
    far_signal(1)
    for c in gcopies:
        c.wait_recv()
    pcopy = pltpu.make_async_copy(pv, psm, psem)
    pcopy.start()

    patf = pv[...].astype(jnp.float32).reshape(32, 128)
    lanes32 = lax.broadcasted_iota(jnp.int32, (32, 128), 1)
    for j in range(2):
        col = jnp.sum(jnp.where(lanes32 == 2 * blk + j, patf, 0.0), axis=1, keepdims=True)
        hit = jnp.where(lanes32.astype(jnp.float32) == col, 1.0, 0.0)
        stage[32 * j : 32 * j + 32] = hit
        stage[64 + 32 * j : 96 + 32 * j] = hit
    hot = stage[...].T[0:32]
    oht[:, 0:128] = hot.astype(jnp.bfloat16)
    oht[:, 128:256] = jnp.where(lanes32 < 64, hot, 0.0).astype(jnp.bfloat16)
    weight = wv[...].reshape(32, 128)

    def eight_sums(terms):
        total = terms[0:8]
        for k in range(1, 16):
            total = total + terms[8 * k : 8 * k + 8]
        return total

    def group_rows(slot):
        total = part[slot, pl.ds(0, 8, stride=8), :]
        for k in range(1, 8):
            total = total + part[slot, pl.ds(k, 8, stride=8), :]
        return total

    def backward_tiles(first, rows, square, beside=()):
        for t in range(first, first + rows.shape[0]):
            for copy in beside[EACH * (t - first) : EACH * (t - first) + EACH]:
                copy.start()
            wc = jnp.broadcast_to(rows[t - first : t - first + 1], (128, 128)).T
            for j in range(2):
                tile = jac[t, j]
                term = tile * wc
                if square:
                    term = term * tile
                part[4 * j + t // 8, 8 * (t % 8) : 8 * (t % 8) + 8] = eight_sums(term)

    def backward_end(par):
        whole = jnp.concatenate([group_rows(k) for k in range(8)], axis=0)
        high = whole.astype(jnp.bfloat16)
        rest = whole - high.astype(jnp.float32)
        mid = rest.astype(jnp.bfloat16)
        low = (rest - mid.astype(jnp.float32)).astype(jnp.bfloat16)
        stack = jnp.concatenate([high, mid, low, jnp.zeros((64, 128), jnp.bfloat16)], axis=0)
        total = jnp.dot(oht[...], stack, preferred_element_type=jnp.float32)
        csend[par] = total[0:24]

    def r_copies(par):
        return [
            remote(csend.at[par, pl.ds(16, 8)], rlo8.at[par], rsend.at[par], rrecv.at[par], to_reg(2)),
            remote(csend.at[par, pl.ds(0, 8)], rhi8.at[par], rsend.at[par], rrecv.at[par], to_reg(-2)),
            remote(csend.at[par, pl.ds(8, 16)], rlo16.at[par], rsend.at[par], rrecv.at[par], to_reg(1)),
            remote(csend.at[par, pl.ds(0, 16)], rhi16.at[par], rsend.at[par], rrecv.at[par], to_reg(-1)),
        ]

    def r_whole(par):
        return whole(xbuf.at[par, pl.ds(0, 2), pl.ds(0, 24)], rsend.at[par], rrecv.at[par])

    def r_sum(par):
        before = rlo8[par] + rlo16[par, 0:8] + csend[par, 0:8]
        own = rlo16[par, 8:16] + csend[par, 8:16] + rhi16[par, 0:8]
        after = csend[par, 16:24] + rhi16[par, 8:16] + rhi8[par]
        return jnp.concatenate([before, own, after], axis=0)

    for c in jcopies:
        c.wait()
    backward_tiles(0, weight, True)
    backward_end(0)
    copies = r_copies(0)
    for c in copies:
        c.start()
    pl.semaphore_wait(far_sem.at[1], 2)
    far_signal(2)
    pcopy.wait()
    for c in hcopies:
        c.wait_recv()
    copies = [r_whole(0)]
    copies[0].wait_recv()
    diag[...] = jnp.concatenate([hbuf[0, 0:8], hsend[0:8], hbuf[1, 0:8]], axis=0)
    resid0 = jnp.concatenate([hbuf[0, 8:16], hsend[8:16], hbuf[1, 8:16]], axis=0)
    inv = 1.0 / (diag[...] + r_sum(0))
    for c in copies + gcopies + hcopies:
        c.wait_send()
    pl.semaphore_wait(far_sem.at[2], 2)

    offsets = [(z, y, c) for z in range(n_reg // 8) for y in range(4) for c in range(2)][1:]
    order = sorted(offsets, key=farness, reverse=True)

    def to_offset(offset):
        z, y, c = offset
        there_z = lax.rem(reg // 8 + z, n_reg // 8)
        there_y = lax.rem(lax.rem(reg // 2, 4) + y, 4)
        return ((there_z * 4 + there_y) * 2 + lax.rem(reg + c, 2), blk)

    zeros8 = jnp.zeros((8, 128), jnp.float32)
    zeros24 = jnp.zeros((24, 128), jnp.float32)
    none = jnp.zeros((1, 1), jnp.float32)

    def step(i, carry):
        solution, direction, resid, along, over_gamma, over_alpha = carry
        par = lax.rem(i, 2)
        rpar = lax.rem(i + 1, 2)
        scaled = inv * resid
        uv[...] = scaled
        own_u = scaled[8:16]
        first = jnp.sum(own_u * resid[8:16], axis=0, keepdims=True)
        second = jnp.sum(own_u * own_u * diag[8:16], axis=0, keepdims=True)
        xbuf[par, blk, SPAN : SPAN + 1] = first
        xbuf[par, blk, SPAN + 1 : SPAN + 2] = second

        xcopies = []
        for c in range(CHUNKS):
            for t in range(SPAN * c, SPAN * c + SPAN):
                if c and t == SPAN * c + INTO:
                    for copy in xcopies[c - 1]:
                        copy.start()
                x0 = uv[pl.ds(psm[t // 8, t % 8, 2 * blk], 1), :]
                x1 = uv[pl.ds(psm[t // 8, t % 8, 2 * blk + 1], 1), :]
                both = jac[t, 0] * x0 + jac[t, 1] * x1
                part[t // 8, 8 * (t % 8) : 8 * (t % 8) + 8] = eight_sums(both.T)
            at = SPAN * c + (8 if c else 0)
            for g in range(SPAN // 8):
                xbuf[par, blk, at + 8 * g : at + 8 * g + 8] = group_rows(SPAN // 8 * c + g)
            mine = xbuf.at[par, blk, pl.ds(at, SPAN if c else SPAN + 2)]
            xcopies.append([
                remote(mine, mine, xsend.at[par], xrecv.at[par, c], to_blk(k))
                for k in (2, 1, 3)
            ])
        for copy in xcopies[-1]:
            copy.start()
        energy = jnp.zeros((1, 128), jnp.float32)
        for c in range(CHUNKS):
            at = SPAN * c + (8 if c else 0)
            landed = xbuf.at[par, pl.ds(0, n_blk - 1), pl.ds(at, SPAN if c else SPAN + 2)]
            whole(landed, xsend.at[par], xrecv.at[par, c]).wait_recv()
            b0, b1, b2, b3 = (xbuf[par, b, at : at + SPAN] for b in range(4))
            rows = b0 + b1 + b2 + b3
            weighted = weight[SPAN * c : SPAN * c + SPAN] * rows
            energy = energy + jnp.sum(weighted * rows, axis=0, keepdims=True)
            if c < CHUNKS - 1:
                backward_tiles(SPAN * c, weighted, False)
        b0, b1, b2, b3 = (xbuf[par, b, SPAN : SPAN + 2] for b in range(4))
        row = lax.broadcasted_iota(jnp.int32, (2, 128), 0)
        dbuf[par, reg] = b0 + b1 + b2 + b3 + jnp.where(row == 1, energy, 0.0)
        dcopies = [
            remote(dbuf.at[par, reg], dbuf.at[par, reg], dsend.at[par], drecv.at[par], to_offset(k))
            for k in order
        ]
        backward_tiles(32 - SPAN, weighted, False, dcopies[:EARLY])
        backward_end(rpar)
        rcopies = r_copies(rpar)
        for c in rcopies + dcopies[EARLY:]:
            c.start()
        rall = r_whole(rpar)
        rall.wait_recv()
        image = diag[...] * scaled + r_sum(rpar)
        others = dbuf.at[par, pl.ds(0, n_reg - 1)]
        dall = remote(others, others, dsend.at[par], drecv.at[par], to_reg(1))
        dall.wait_recv()
        sums = jnp.sum(jnp.sum(dbuf[par], axis=0), axis=1, keepdims=True)
        gamma, delta = sums[0:1], sums[1:2]
        beta = gamma * over_gamma
        alpha = gamma / (delta - beta * gamma * over_alpha)
        direction = own_u + beta * direction
        along = image + beta * along
        out_ref[0:8] = solution
        out_ref[8:16] = direction
        out_ref[16:24] = resid[8:16]
        out_ref[24:32] = along[8:16]
        out_ref[32:40] = jnp.broadcast_to(alpha, (8, 128))
        solution = solution + alpha * direction
        resid = resid - alpha * along
        sent = xbuf.at[par, pl.ds(0, n_blk - 1), pl.ds(0, 34)]
        xall = whole(sent, xsend.at[par], xrecv.at[par, 0])
        for c in (xall, rall, dall):
            c.wait_send()
        return (solution, direction, resid, along, 1.0 / gamma, 1.0 / alpha)

    lax.fori_loop(0, ITERS, step, (zeros8, zeros8, resid0, zeros24, none, none))


def solution(mesh):
    n_reg, n_blk = mesh.shape["region"], mesh.shape["blk"]
    f32 = jnp.float32

    def body(jac_bus, pattern, branch_weight, bus_diag, right_side):
        vmem = pl.BlockSpec(memory_space=pltpu.VMEM)
        shape = jax.ShapeDtypeStruct((40, 128), f32)
        dma = pltpu.SemaphoreType.DMA

        def call(*args):
            return kernel(n_reg, n_blk, *args)

        last = pl.pallas_call(
            call,
            out_shape=shape,
            in_specs=[pl.BlockSpec(memory_space=pl.ANY)] * 5,
            out_specs=vmem,
            scratch_shapes=[
                pltpu.VMEM((32, 2, 128, 128), f32),
                pltpu.VMEM((8, 8), jnp.int32),
                pltpu.VMEM((4, 8, 128), jnp.int32),
                pltpu.SMEM((4, 8, 128), jnp.int32),
                pltpu.VMEM((4, 8, 128), f32),
                pltpu.VMEM((16, 128), f32),
                pltpu.VMEM((2, 16, 128), f32),
                pltpu.VMEM((32, 256), jnp.bfloat16),
                pltpu.VMEM((128, 128), f32),
                pltpu.VMEM((8, 64, 128), f32),
                pltpu.VMEM((24, 128), f32),
                pltpu.VMEM((24, 128), f32),
                pltpu.VMEM((2, 4, 40, 128), f32),
                pltpu.VMEM((2, 24, 128), f32),
                pltpu.VMEM((2, 16, 128), f32),
                pltpu.VMEM((2, 16, 128), f32),
                pltpu.VMEM((2, 8, 128), f32),
                pltpu.VMEM((2, 8, 128), f32),
                pltpu.VMEM((2, 32, 2, 128), f32),
                dma, dma((2,)), pltpu.SemaphoreType.REGULAR((3,)), dma, dma((2,)), dma((2,)), dma, dma,
                dma((2,)), dma((2, CHUNKS)), dma((2,)), dma((2,)), dma((2,)), dma((2,)),
            ],
            compiler_params=pltpu.CompilerParams(collective_id=0, has_side_effects=True),
            name="pcg",
        )(jac_bus, pattern, branch_weight, bus_diag, right_side)
        before, direction, resid, along, alpha = (last[8 * k : 8 * k + 8] for k in range(5))
        return before + alpha * direction, resid - alpha * along

    axes = ("region", "blk")
    in_specs = (P("region", "blk", None, None),) + (P(axes, None),) * 4
    return jax.shard_map(
        body, mesh=mesh, in_specs=in_specs, out_specs=(P(axes, None),) * 2, check_vma=False
    )
```

```python
import jax
import jax.numpy as jnp
from jax import lax
from jax.experimental import pallas as pl
from jax.experimental.pallas import tpu as pltpu
from jax.sharding import PartitionSpec as P

ITERS = 12
EARLY = 18
EACH = 18
INTO = 1
CHUNKS = 2
SPAN = 32 // CHUNKS
MESH = pl.DeviceIdType.MESH


def farness(offset):
    steps = [min(n, 4 - n) for n in offset[:2]]
    return (min(steps) > 0, sum(steps), offset[2] == 0)


def kernel(
    n_reg, n_blk,
    jac_hbm, pattern_hbm, weight_hbm, diag_hbm, rhs_hbm,
    out_ref,
    jac, pat, pv, psm, wv, hsend, hbuf, oht, stage, part, uv, qv, diag, xbuf, csend, rlo16, rhi16, rlo8, rhi8, dbuf,
    jsem, isem, far_sem, psem, gsend, grecv, hsend_sem, hrecv, xsend, xrecv, rsend, rrecv, dsend, drecv,
):
    reg = lax.axis_index("region")
    blk = lax.axis_index("blk")

    def region_at(k):
        return lax.rem(reg + k + n_reg, n_reg)

    def blk_at(k):
        return lax.rem(blk + k, n_blk)

    def to_blk(k):
        return (reg, blk_at(k))

    def to_reg(k):
        return (region_at(k), blk)

    def remote(src, dst, ssem, rsem, dev):
        return pltpu.make_async_remote_copy(
            src_ref=src, dst_ref=dst, send_sem=ssem, recv_sem=rsem,
            device_id=dev, device_id_type=MESH,
        )

    jcopies = [
        pltpu.make_async_copy(jac_hbm, jac, jsem)
        for _ in range(1)
    ]
    icopies = [
        pltpu.make_async_copy(pattern_hbm, pat, isem.at[1]),
        pltpu.make_async_copy(weight_hbm, wv.at[blk], isem.at[0]),
        pltpu.make_async_copy(diag_hbm, hsend.at[pl.ds(0, 8)], isem.at[0]),
        pltpu.make_async_copy(rhs_hbm, hsend.at[pl.ds(8, 8)], isem.at[0]),
    ]
    for c in icopies + jcopies:
        c.start()

    barrier = pltpu.get_barrier_semaphore()
    near = [to_blk(k) for k in range(1, n_blk)] + [to_reg(k) for k in (1, -1, 2, -2)]
    for dev in near:
        pl.semaphore_signal(barrier, inc=1, device_id=dev, device_id_type=MESH)

    def far_signal(n):
        for k in (2 << n, -(2 << n)):
            pl.semaphore_signal(far_sem.at[n], inc=1, device_id=to_reg(k), device_id_type=MESH)

    pv[blk] = jnp.zeros((8, 128), jnp.int32)
    icopies[0].wait()
    landed = stage.at[pl.ds(0, 24)]
    pltpu.make_async_copy(landed, landed, isem.at[0]).wait()
    pv[blk, :, 0:8] = pat[...]
    pl.semaphore_wait(barrier, len(near))

    gcopies = []
    for k in range(1, n_blk):
        gcopies.append(remote(pv.at[blk], pv.at[blk], gsend.at[0], grecv.at[0], to_blk(k)))
        gcopies.append(remote(wv.at[blk], wv.at[blk], gsend.at[1], grecv.at[1], to_blk(k)))
    hcopies = [
        remote(hsend, hbuf.at[0], hsend_sem, hrecv, to_reg(1)),
        remote(hsend, hbuf.at[1], hsend_sem, hrecv, to_reg(-1)),
    ]
    for c in gcopies + hcopies:
        c.start()

    def whole(ref, ssem, rsem):
        return remote(ref, ref, ssem, rsem, to_blk(1))

    gcopies = [
        whole(pv.at[pl.ds(0, n_blk - 1)], gsend.at[0], grecv.at[0]),
        whole(wv.at[pl.ds(0, n_blk - 1)], gsend.at[1], grecv.at[1]),
    ]
    hcopies = [whole(hbuf, hsend_sem, hrecv)]
    far_signal(0)
    pl.semaphore_wait(far_sem.at[0], 2)
    far_signal(1)
    for c in gcopies:
        c.wait_recv()
    pcopy = pltpu.make_async_copy(pv, psm, psem)
    pcopy.start()

    patf = pv[...].astype(jnp.float32).reshape(32, 128)
    lanes32 = lax.broadcasted_iota(jnp.int32, (32, 128), 1)
    for j in range(2):
        col = jnp.sum(jnp.where(lanes32 == 2 * blk + j, patf, 0.0), axis=1, keepdims=True)
        hit = jnp.where(lanes32.astype(jnp.float32) == col, 1.0, 0.0)
        stage[32 * j : 32 * j + 32] = hit
        stage[64 + 32 * j : 96 + 32 * j] = hit
    hot = stage[...].T[0:32]
    oht[:, 0:128] = hot.astype(jnp.bfloat16)
    oht[:, 128:256] = jnp.where(lanes32 < 64, hot, 0.0).astype(jnp.bfloat16)
    weight = wv[...].reshape(32, 128)

    def eight_sums(terms):
        total = terms[0:8]
        for k in range(1, 16):
            total = total + terms[8 * k : 8 * k + 8]
        return total

    def group_rows(slot):
        total = part[slot, pl.ds(0, 8, stride=8), :]
        for k in range(1, 8):
            total = total + part[slot, pl.ds(k, 8, stride=8), :]
        return total

    def backward_tiles(first, rows, square, beside=()):
        for t in range(first, first + rows.shape[0]):
            for copy in beside[EACH * (t - first) : EACH * (t - first) + EACH]:
                copy.start()
            wc = jnp.broadcast_to(rows[t - first : t - first + 1], (128, 128)).T
            for j in range(2):
                tile = jac[t, j]
                term = tile * wc
                if square:
                    term = term * tile
                part[4 * j + t // 8, 8 * (t % 8) : 8 * (t % 8) + 8] = eight_sums(term)

    def backward_end(par):
        whole = jnp.concatenate([group_rows(k) for k in range(8)], axis=0)
        high = whole.astype(jnp.bfloat16)
        rest = whole - high.astype(jnp.float32)
        mid = rest.astype(jnp.bfloat16)
        low = (rest - mid.astype(jnp.float32)).astype(jnp.bfloat16)
        stack = jnp.concatenate([high, mid, low, jnp.zeros((64, 128), jnp.bfloat16)], axis=0)
        total = jnp.dot(oht[...], stack, preferred_element_type=jnp.float32)
        csend[par] = total[0:24]

    def r_copies(par):
        return [
            remote(csend.at[par, pl.ds(16, 8)], rlo8.at[par], rsend.at[par], rrecv.at[par], to_reg(2)),
            remote(csend.at[par, pl.ds(0, 8)], rhi8.at[par], rsend.at[par], rrecv.at[par], to_reg(-2)),
            remote(csend.at[par, pl.ds(8, 16)], rlo16.at[par], rsend.at[par], rrecv.at[par], to_reg(1)),
            remote(csend.at[par, pl.ds(0, 16)], rhi16.at[par], rsend.at[par], rrecv.at[par], to_reg(-1)),
        ]

    def r_whole(par):
        return whole(xbuf.at[par, pl.ds(0, 2), pl.ds(0, 24)], rsend.at[par], rrecv.at[par])

    def r_sum(par):
        before = rlo8[par] + rlo16[par, 0:8] + csend[par, 0:8]
        own = rlo16[par, 8:16] + csend[par, 8:16] + rhi16[par, 0:8]
        after = csend[par, 16:24] + rhi16[par, 8:16] + rhi8[par]
        return jnp.concatenate([before, own, after], axis=0)

    for c in jcopies:
        c.wait()
    backward_tiles(0, weight, True)
    backward_end(0)
    copies = r_copies(0)
    for c in copies:
        c.start()
    pl.semaphore_wait(far_sem.at[1], 2)
    far_signal(2)
    pcopy.wait()
    for c in hcopies:
        c.wait_recv()
    copies = [r_whole(0)]
    copies[0].wait_recv()
    diag[...] = jnp.concatenate([hbuf[0, 0:8], hsend[0:8], hbuf[1, 0:8]], axis=0)
    resid0 = jnp.concatenate([hbuf[0, 8:16], hsend[8:16], hbuf[1, 8:16]], axis=0)
    inv = 1.0 / (diag[...] + r_sum(0))
    for c in copies + gcopies + hcopies:
        c.wait_send()
    pl.semaphore_wait(far_sem.at[2], 2)

    offsets = [(z, y, c) for z in range(n_reg // 8) for y in range(4) for c in range(2)][1:]
    order = sorted(offsets, key=farness, reverse=True)

    def to_offset(offset):
        z, y, c = offset
        there_z = lax.rem(reg // 8 + z, n_reg // 8)
        there_y = lax.rem(lax.rem(reg // 2, 4) + y, 4)
        return ((there_z * 4 + there_y) * 2 + lax.rem(reg + c, 2), blk)

    zeros8 = jnp.zeros((8, 128), jnp.float32)
    zeros24 = jnp.zeros((24, 128), jnp.float32)
    none = jnp.zeros((1, 1), jnp.float32)

    def forward_tiles(source_ref, c, before=()):
        for t in range(SPAN * c, SPAN * c + SPAN):
            if t == SPAN * c + INTO:
                for copy in before:
                    copy.start()
            x0 = source_ref[pl.ds(psm[t // 8, t % 8, 2 * blk], 1), :]
            x1 = source_ref[pl.ds(psm[t // 8, t % 8, 2 * blk + 1], 1), :]
            both = jac[t, 0] * x0 + jac[t, 1] * x1
            part[t // 8, 8 * (t % 8) : 8 * (t % 8) + 8] = eight_sums(both.T)
        return jnp.concatenate([group_rows(SPAN // 8 * c + g) for g in range(SPAN // 8)], axis=0)

    def chunk_at(c):
        return SPAN * c + (8 if c else 0)

    def place(par, c, rows):
        xbuf[par, blk, chunk_at(c) : chunk_at(c) + SPAN] = rows
        mine = xbuf.at[par, blk, pl.ds(chunk_at(c), SPAN if c else SPAN + 2)]
        return [remote(mine, mine, xsend.at[par], xrecv.at[par, c], to_blk(k)) for k in (2, 1, 3)]

    def place_sums(par, own_u, own_r):
        first = jnp.sum(own_u * own_r, axis=0, keepdims=True)
        second = jnp.sum(own_u * own_u * diag[8:16], axis=0, keepdims=True)
        xbuf[par, blk, SPAN : SPAN + 1] = first
        xbuf[par, blk, SPAN + 1 : SPAN + 2] = second

    def bus_sums(par, rpar, wide):
        energy = jnp.zeros((1, 128), jnp.float32)
        for c in range(CHUNKS):
            at = chunk_at(c)
            landed = xbuf.at[par, pl.ds(0, n_blk - 1), pl.ds(at, SPAN if c else SPAN + 2)]
            whole(landed, xsend.at[par], xrecv.at[par, c]).wait_recv()
            b0, b1, b2, b3 = (xbuf[par, b, at : at + SPAN] for b in range(4))
            rows = b0 + b1 + b2 + b3
            weighted = weight[SPAN * c : SPAN * c + SPAN] * rows
            energy = energy + jnp.sum(weighted * rows, axis=0, keepdims=True)
            if c < CHUNKS - 1:
                backward_tiles(SPAN * c, weighted, False)
        b0, b1, b2, b3 = (xbuf[par, b, SPAN : SPAN + 2] for b in range(4))
        row = lax.broadcasted_iota(jnp.int32, (2, 128), 0)
        dbuf[par, reg] = b0 + b1 + b2 + b3 + jnp.where(row == 1, energy, 0.0)
        dcopies = [
            remote(dbuf.at[par, reg], dbuf.at[par, reg], dsend.at[par], drecv.at[par], to_offset(k))
            for k in order
        ]
        backward_tiles(32 - SPAN, weighted, False, dcopies[:EARLY])
        backward_end(rpar)
        for c in r_copies(rpar)[0 if wide else 2 :] + dcopies[EARLY:]:
            c.start()
        others = dbuf.at[par, pl.ds(0, n_reg - 1)]
        return whole(others, dsend.at[par], drecv.at[par])

    def scalars(par, over_gamma, over_alpha):
        sums = jnp.sum(jnp.sum(dbuf[par], axis=0), axis=1, keepdims=True)
        gamma, delta = sums[0:1], sums[1:2]
        beta = gamma * over_gamma
        alpha = gamma / (delta - beta * gamma * over_alpha)
        return gamma, alpha, beta

    def sent_whole(par):
        sent = xbuf.at[par, pl.ds(0, n_blk - 1), pl.ds(0, 34)]
        return whole(sent, xsend.at[par], xrecv.at[par, 0])

    uv[...] = inv * resid0
    place_sums(0, uv[8:16], resid0[8:16])
    for c in range(CHUNKS):
        for copy in place(0, c, forward_tiles(uv, c)):
            copy.start()

    def step(i, carry):
        solution, direction, resid, along, over_gamma, over_alpha = carry
        par = lax.rem(i, 2)
        rpar = lax.rem(i + 1, 2)
        scaled = inv * resid
        uv[...] = scaled
        qv[...] = inv * along
        dall = bus_sums(par, rpar, True)
        kept_u = [forward_tiles(uv, c) for c in range(CHUNKS)]
        kept_q = [forward_tiles(qv, c) for c in range(CHUNKS)]
        rall = r_whole(rpar)
        rall.wait_recv()
        image = diag[...] * scaled + r_sum(rpar)
        uv[...] = inv * image
        fresh = forward_tiles(uv, 0)
        dall.wait_recv()
        gamma, alpha, beta = scalars(par, over_gamma, over_alpha)
        direction = scaled[8:16] + beta * direction
        along = image + beta * along
        solution = solution + alpha * direction
        resid = resid - alpha * along
        place_sums(rpar, inv[8:16] * resid[8:16], resid[8:16])
        copies = place(rpar, 0, kept_u[0] - alpha * (fresh + beta * kept_q[0]))
        for c in range(1, CHUNKS):
            fresh = forward_tiles(uv, c, copies)
            copies = place(rpar, c, kept_u[c] - alpha * (fresh + beta * kept_q[c]))
        for copy in copies:
            copy.start()
        for c in (sent_whole(par), rall, dall):
            c.wait_send()
        return (solution, direction, resid, along, 1.0 / gamma, 1.0 / alpha)

    carry = lax.fori_loop(0, ITERS - 1, step, (zeros8, zeros8, resid0, zeros24, none, none))
    solution, direction, resid, along, over_gamma, over_alpha = carry
    par, rpar = (ITERS - 1) % 2, ITERS % 2
    dall = bus_sums(par, rpar, False)
    rall = whole(xbuf.at[rpar, pl.ds(0, 2), pl.ds(0, 16)], rsend.at[rpar], rrecv.at[rpar])
    rall.wait_recv()
    scaled = inv[8:16] * resid[8:16]
    image = diag[8:16] * scaled + (rlo16[rpar, 8:16] + csend[rpar, 8:16] + rhi16[rpar, 0:8])
    dall.wait_recv()
    gamma, alpha, beta = scalars(par, over_gamma, over_alpha)
    out_ref[0:8] = solution
    out_ref[8:16] = scaled + beta * direction
    out_ref[16:24] = resid[8:16]
    out_ref[24:32] = image + beta * along[8:16]
    out_ref[32:40] = jnp.broadcast_to(alpha, (8, 128))
    for c in (sent_whole(par), rall, dall):
        c.wait_send()


def solution(mesh):
    n_reg, n_blk = mesh.shape["region"], mesh.shape["blk"]
    f32 = jnp.float32

    def body(jac_bus, pattern, branch_weight, bus_diag, right_side):
        vmem = pl.BlockSpec(memory_space=pltpu.VMEM)
        shape = jax.ShapeDtypeStruct((40, 128), f32)
        dma = pltpu.SemaphoreType.DMA

        def call(*args):
            return kernel(n_reg, n_blk, *args)

        last = pl.pallas_call(
            call,
            out_shape=shape,
            in_specs=[pl.BlockSpec(memory_space=pl.ANY)] * 5,
            out_specs=vmem,
            scratch_shapes=[
                pltpu.VMEM((32, 2, 128, 128), f32),
                pltpu.VMEM((8, 8), jnp.int32),
                pltpu.VMEM((4, 8, 128), jnp.int32),
                pltpu.SMEM((4, 8, 128), jnp.int32),
                pltpu.VMEM((4, 8, 128), f32),
                pltpu.VMEM((16, 128), f32),
                pltpu.VMEM((2, 16, 128), f32),
                pltpu.VMEM((32, 256), jnp.bfloat16),
                pltpu.VMEM((128, 128), f32),
                pltpu.VMEM((8, 64, 128), f32),
                pltpu.VMEM((24, 128), f32),
                pltpu.VMEM((24, 128), f32),
                pltpu.VMEM((24, 128), f32),
                pltpu.VMEM((2, 4, 40, 128), f32),
                pltpu.VMEM((2, 24, 128), f32),
                pltpu.VMEM((2, 16, 128), f32),
                pltpu.VMEM((2, 16, 128), f32),
                pltpu.VMEM((2, 8, 128), f32),
                pltpu.VMEM((2, 8, 128), f32),
                pltpu.VMEM((2, 32, 2, 128), f32),
                dma, dma((2,)), pltpu.SemaphoreType.REGULAR((3,)), dma, dma((2,)), dma((2,)), dma, dma,
                dma((2,)), dma((2, CHUNKS)), dma((2,)), dma((2,)), dma((2,)), dma((2,)),
            ],
            compiler_params=pltpu.CompilerParams(collective_id=0, has_side_effects=True),
            name="pcg",
        )(jac_bus, pattern, branch_weight, bus_diag, right_side)
        before, direction, resid, along, alpha = (last[8 * k : 8 * k + 8] for k in range(5))
        return before + alpha * direction, resid - alpha * along

    axes = ("region", "blk")
    in_specs = (P("region", "blk", None, None),) + (P(axes, None),) * 4
    return jax.shard_map(
        body, mesh=mesh, in_specs=in_specs, out_specs=(P(axes, None),) * 2, check_vma=False
    )
```

```python
import jax
import jax.numpy as jnp
from jax import lax
from jax.experimental import pallas as pl
from jax.experimental.pallas import tpu as pltpu
from jax.sharding import PartitionSpec as P

ITERS = 12
EARLY = 18
EACH = 5
INTO = 1
CHUNKS = 2
SPAN = 32 // CHUNKS
MESH = pl.DeviceIdType.MESH


def farness(offset):
    steps = [min(n, 4 - n) for n in offset[:2]]
    return (min(steps) > 0, sum(steps), offset[2] == 0)


def kernel(
    n_reg, n_blk,
    jac_hbm, pattern_hbm, weight_hbm, diag_hbm, rhs_hbm,
    out_ref,
    jac, pat, pv, psm, wv, hsend, hbuf, oht, stage, part, uv, qv, diag, xbuf, csend, rlo16, rhi16, rlo8, rhi8, dbuf,
    jsem, isem, far_sem, psem, gsend, grecv, hsend_sem, hrecv, xsend, xrecv, rsend, rrecv, dsend, drecv,
):
    reg = lax.axis_index("region")
    blk = lax.axis_index("blk")

    def region_at(k):
        return lax.rem(reg + k + n_reg, n_reg)

    def blk_at(k):
        return lax.rem(blk + k, n_blk)

    def to_blk(k):
        return (reg, blk_at(k))

    def to_reg(k):
        return (region_at(k), blk)

    def remote(src, dst, ssem, rsem, dev):
        return pltpu.make_async_remote_copy(
            src_ref=src, dst_ref=dst, send_sem=ssem, recv_sem=rsem,
            device_id=dev, device_id_type=MESH,
        )

    jcopies = [
        pltpu.make_async_copy(jac_hbm, jac, jsem)
        for _ in range(1)
    ]
    icopies = [
        pltpu.make_async_copy(pattern_hbm, pat, isem.at[1]),
        pltpu.make_async_copy(weight_hbm, wv.at[blk], isem.at[0]),
        pltpu.make_async_copy(diag_hbm, hsend.at[pl.ds(0, 8)], isem.at[0]),
        pltpu.make_async_copy(rhs_hbm, hsend.at[pl.ds(8, 8)], isem.at[0]),
    ]
    for c in icopies + jcopies:
        c.start()

    barrier = pltpu.get_barrier_semaphore()
    near = [to_blk(k) for k in range(1, n_blk)] + [to_reg(k) for k in (1, -1, 2, -2)]
    for dev in near:
        pl.semaphore_signal(barrier, inc=1, device_id=dev, device_id_type=MESH)

    def far_signal(n):
        for k in (2 << n, -(2 << n)):
            pl.semaphore_signal(far_sem.at[n], inc=1, device_id=to_reg(k), device_id_type=MESH)

    pv[blk] = jnp.zeros((8, 128), jnp.int32)
    icopies[0].wait()
    landed = stage.at[pl.ds(0, 24)]
    pltpu.make_async_copy(landed, landed, isem.at[0]).wait()
    pv[blk, :, 0:8] = pat[...]
    pl.semaphore_wait(barrier, len(near))

    gcopies = []
    for k in range(1, n_blk):
        gcopies.append(remote(pv.at[blk], pv.at[blk], gsend.at[0], grecv.at[0], to_blk(k)))
        gcopies.append(remote(wv.at[blk], wv.at[blk], gsend.at[1], grecv.at[1], to_blk(k)))
    hcopies = [
        remote(hsend, hbuf.at[0], hsend_sem, hrecv, to_reg(1)),
        remote(hsend, hbuf.at[1], hsend_sem, hrecv, to_reg(-1)),
    ]
    for c in gcopies + hcopies:
        c.start()

    def whole(ref, ssem, rsem):
        return remote(ref, ref, ssem, rsem, to_blk(1))

    gcopies = [
        whole(pv.at[pl.ds(0, n_blk - 1)], gsend.at[0], grecv.at[0]),
        whole(wv.at[pl.ds(0, n_blk - 1)], gsend.at[1], grecv.at[1]),
    ]
    hcopies = [whole(hbuf, hsend_sem, hrecv)]
    far_signal(0)
    pl.semaphore_wait(far_sem.at[0], 2)
    far_signal(1)
    for c in gcopies:
        c.wait_recv()
    pcopy = pltpu.make_async_copy(pv, psm, psem)
    pcopy.start()

    patf = pv[...].astype(jnp.float32).reshape(32, 128)
    lanes32 = lax.broadcasted_iota(jnp.int32, (32, 128), 1)
    for j in range(2):
        col = jnp.sum(jnp.where(lanes32 == 2 * blk + j, patf, 0.0), axis=1, keepdims=True)
        hit = jnp.where(lanes32.astype(jnp.float32) == col, 1.0, 0.0)
        stage[32 * j : 32 * j + 32] = hit
        stage[64 + 32 * j : 96 + 32 * j] = hit
    hot = stage[...].T[0:32]
    oht[:, 0:128] = hot.astype(jnp.bfloat16)
    oht[:, 128:256] = jnp.where(lanes32 < 64, hot, 0.0).astype(jnp.bfloat16)
    weight = wv[...].reshape(32, 128)

    def eight_sums(terms):
        total = terms[0:8]
        for k in range(1, 16):
            total = total + terms[8 * k : 8 * k + 8]
        return total

    def group_rows(slot):
        total = part[slot, pl.ds(0, 8, stride=8), :]
        for k in range(1, 8):
            total = total + part[slot, pl.ds(k, 8, stride=8), :]
        return total

    def backward_tiles(first, rows, square, beside=()):
        for t in range(first, first + rows.shape[0]):
            for copy in beside[EACH * (t - first) : EACH * (t - first) + EACH]:
                copy.start()
            wc = jnp.broadcast_to(rows[t - first : t - first + 1], (128, 128)).T
            for j in range(2):
                tile = jac[t, j]
                term = tile * wc
                if square:
                    term = term * tile
                part[4 * j + t // 8, 8 * (t % 8) : 8 * (t % 8) + 8] = eight_sums(term)

    def backward_end(par):
        whole = jnp.concatenate([group_rows(k) for k in range(8)], axis=0)
        high = whole.astype(jnp.bfloat16)
        rest = whole - high.astype(jnp.float32)
        mid = rest.astype(jnp.bfloat16)
        low = (rest - mid.astype(jnp.float32)).astype(jnp.bfloat16)
        stack = jnp.concatenate([high, mid, low, jnp.zeros((64, 128), jnp.bfloat16)], axis=0)
        total = jnp.dot(oht[...], stack, preferred_element_type=jnp.float32)
        csend[par] = total[0:24]

    def r_copies(par):
        return [
            remote(csend.at[par, pl.ds(16, 8)], rlo8.at[par], rsend.at[par], rrecv.at[par], to_reg(2)),
            remote(csend.at[par, pl.ds(0, 8)], rhi8.at[par], rsend.at[par], rrecv.at[par], to_reg(-2)),
            remote(csend.at[par, pl.ds(8, 16)], rlo16.at[par], rsend.at[par], rrecv.at[par], to_reg(1)),
            remote(csend.at[par, pl.ds(0, 16)], rhi16.at[par], rsend.at[par], rrecv.at[par], to_reg(-1)),
        ]

    def r_whole(par):
        return whole(xbuf.at[par, pl.ds(0, 2), pl.ds(0, 24)], rsend.at[par], rrecv.at[par])

    def r_sum(par):
        before = rlo8[par] + rlo16[par, 0:8] + csend[par, 0:8]
        own = rlo16[par, 8:16] + csend[par, 8:16] + rhi16[par, 0:8]
        after = csend[par, 16:24] + rhi16[par, 8:16] + rhi8[par]
        return jnp.concatenate([before, own, after], axis=0)

    for c in jcopies:
        c.wait()
    backward_tiles(0, weight, True)
    backward_end(0)
    copies = r_copies(0)
    for c in copies:
        c.start()
    pl.semaphore_wait(far_sem.at[1], 2)
    far_signal(2)
    pcopy.wait()
    for c in hcopies:
        c.wait_recv()
    copies = [r_whole(0)]
    copies[0].wait_recv()
    diag[...] = jnp.concatenate([hbuf[0, 0:8], hsend[0:8], hbuf[1, 0:8]], axis=0)
    resid0 = jnp.concatenate([hbuf[0, 8:16], hsend[8:16], hbuf[1, 8:16]], axis=0)
    inv = 1.0 / (diag[...] + r_sum(0))
    for c in copies + gcopies + hcopies:
        c.wait_send()
    pl.semaphore_wait(far_sem.at[2], 2)

    offsets = [(z, y, c) for z in range(n_reg // 8) for y in range(4) for c in range(2)][1:]
    order = sorted(offsets, key=farness, reverse=True)

    def to_offset(offset):
        z, y, c = offset
        there_z = lax.rem(reg // 8 + z, n_reg // 8)
        there_y = lax.rem(lax.rem(reg // 2, 4) + y, 4)
        return ((there_z * 4 + there_y) * 2 + lax.rem(reg + c, 2), blk)

    zeros8 = jnp.zeros((8, 128), jnp.float32)
    zeros24 = jnp.zeros((24, 128), jnp.float32)
    none = jnp.zeros((1, 1), jnp.float32)

    def forward_tiles(source_ref, c, before=()):
        for t in range(SPAN * c, SPAN * c + SPAN):
            if t == SPAN * c + INTO:
                for copy in before:
                    copy.start()
            x0 = source_ref[pl.ds(psm[t // 8, t % 8, 2 * blk], 1), :]
            x1 = source_ref[pl.ds(psm[t // 8, t % 8, 2 * blk + 1], 1), :]
            both = jac[t, 0] * x0 + jac[t, 1] * x1
            part[t // 8, 8 * (t % 8) : 8 * (t % 8) + 8] = eight_sums(both.T)
        return jnp.concatenate([group_rows(SPAN // 8 * c + g) for g in range(SPAN // 8)], axis=0)

    def chunk_at(c):
        return SPAN * c + (8 if c else 0)

    def place(par, c, rows):
        xbuf[par, blk, chunk_at(c) : chunk_at(c) + SPAN] = rows
        mine = xbuf.at[par, blk, pl.ds(chunk_at(c), SPAN if c else SPAN + 2)]
        return [remote(mine, mine, xsend.at[par], xrecv.at[par, c], to_blk(k)) for k in (2, 1, 3)]

    def place_sums(par, own_u, own_r):
        first = jnp.sum(own_u * own_r, axis=0, keepdims=True)
        second = jnp.sum(own_u * own_u * diag[8:16], axis=0, keepdims=True)
        xbuf[par, blk, SPAN : SPAN + 1] = first
        xbuf[par, blk, SPAN + 1 : SPAN + 2] = second

    def bus_sums(par, rpar, wide):
        energy = jnp.zeros((1, 128), jnp.float32)
        low_lanes = lax.broadcasted_iota(jnp.int32, (1, 128), 1) < 64
        for c in range(CHUNKS):
            at = chunk_at(c)
            landed = xbuf.at[par, pl.ds(0, n_blk - 1), pl.ds(at, SPAN if c else SPAN + 2)]
            whole(landed, xsend.at[par], xrecv.at[par, c]).wait_recv()
            b0, b1, b2, b3 = (xbuf[par, b, at : at + (SPAN if c else SPAN + 2)] for b in range(4))
            rows = b0[:SPAN] + b1[:SPAN] + b2[:SPAN] + b3[:SPAN]
            weighted = weight[SPAN * c : SPAN * c + SPAN] * rows
            energy = energy + jnp.sum(weighted * rows, axis=0, keepdims=True)
            if c == 0:
                first = b0[SPAN:] + b1[SPAN:] + b2[SPAN:] + b3[SPAN:]
                first = first + pltpu.roll(first, 64, 1)
                held = jnp.where(low_lanes, first[0:1], first[1:2])
            if c < CHUNKS - 1:
                backward_tiles(SPAN * c, weighted, False)
        dbuf[par, reg] = held + jnp.where(low_lanes, 0.0, energy + pltpu.roll(energy, 64, 1))
        dcopies = [
            remote(dbuf.at[par, reg], dbuf.at[par, reg], dsend.at[par], drecv.at[par], to_offset(k))
            for k in order
        ]
        backward_tiles(32 - SPAN, weighted, False, dcopies[:EARLY])
        backward_end(rpar)
        for c in r_copies(rpar)[0 if wide else 2 :] + dcopies[EARLY:]:
            c.start()
        others = dbuf.at[par, pl.ds(0, n_reg - 1)]
        return whole(others, dsend.at[par], drecv.at[par])

    def scalars(par, over_gamma, over_alpha):
        sums = jnp.sum(dbuf[par], axis=0)
        low_lanes = lax.broadcasted_iota(jnp.int32, (1, 128), 1) < 64
        gamma = jnp.sum(jnp.where(low_lanes, sums, 0.0), axis=1, keepdims=True)
        delta = jnp.sum(jnp.where(low_lanes, 0.0, sums), axis=1, keepdims=True)
        beta = gamma * over_gamma
        alpha = gamma / (delta - beta * gamma * over_alpha)
        return gamma, alpha, beta

    def sent_whole(par):
        sent = xbuf.at[par, pl.ds(0, n_blk - 1), pl.ds(0, 34)]
        return whole(sent, xsend.at[par], xrecv.at[par, 0])

    uv[...] = inv * resid0
    place_sums(0, uv[8:16], resid0[8:16])
    for c in range(CHUNKS):
        for copy in place(0, c, forward_tiles(uv, c)):
            copy.start()

    def step(i, carry):
        solution, direction, resid, along, over_gamma, over_alpha = carry
        par = lax.rem(i, 2)
        rpar = lax.rem(i + 1, 2)
        scaled = inv * resid
        uv[...] = scaled
        qv[...] = inv * along
        dall = bus_sums(par, rpar, True)
        kept_u = [forward_tiles(uv, c) for c in range(CHUNKS)]
        kept_q = [forward_tiles(qv, c) for c in range(CHUNKS)]
        rall = r_whole(rpar)
        rall.wait_recv()
        image = diag[...] * scaled + r_sum(rpar)
        uv[...] = inv * image
        fresh = forward_tiles(uv, 0)
        dall.wait_recv()
        gamma, alpha, beta = scalars(par, over_gamma, over_alpha)
        direction = scaled[8:16] + beta * direction
        along = image + beta * along
        solution = solution + alpha * direction
        resid = resid - alpha * along
        place_sums(rpar, inv[8:16] * resid[8:16], resid[8:16])
        copies = place(rpar, 0, kept_u[0] - alpha * (fresh + beta * kept_q[0]))
        for c in range(1, CHUNKS):
            fresh = forward_tiles(uv, c, copies)
            copies = place(rpar, c, kept_u[c] - alpha * (fresh + beta * kept_q[c]))
        for copy in copies:
            copy.start()
        for c in (sent_whole(par), rall, dall):
            c.wait_send()
        return (solution, direction, resid, along, 1.0 / gamma, 1.0 / alpha)

    carry = lax.fori_loop(0, ITERS - 1, step, (zeros8, zeros8, resid0, zeros24, none, none))
    solution, direction, resid, along, over_gamma, over_alpha = carry
    par, rpar = (ITERS - 1) % 2, ITERS % 2
    dall = bus_sums(par, rpar, False)
    rall = whole(xbuf.at[rpar, pl.ds(0, 2), pl.ds(0, 16)], rsend.at[rpar], rrecv.at[rpar])
    rall.wait_recv()
    scaled = inv[8:16] * resid[8:16]
    image = diag[8:16] * scaled + (rlo16[rpar, 8:16] + csend[rpar, 8:16] + rhi16[rpar, 0:8])
    dall.wait_recv()
    gamma, alpha, beta = scalars(par, over_gamma, over_alpha)
    out_ref[0:8] = solution
    out_ref[8:16] = scaled + beta * direction
    out_ref[16:24] = resid[8:16]
    out_ref[24:32] = image + beta * along[8:16]
    out_ref[32:40] = jnp.broadcast_to(alpha, (8, 128))
    for c in (sent_whole(par), rall, dall):
        c.wait_send()


def solution(mesh):
    n_reg, n_blk = mesh.shape["region"], mesh.shape["blk"]
    f32 = jnp.float32

    def body(jac_bus, pattern, branch_weight, bus_diag, right_side):
        vmem = pl.BlockSpec(memory_space=pltpu.VMEM)
        shape = jax.ShapeDtypeStruct((40, 128), f32)
        dma = pltpu.SemaphoreType.DMA

        def call(*args):
            return kernel(n_reg, n_blk, *args)

        last = pl.pallas_call(
            call,
            out_shape=shape,
            in_specs=[pl.BlockSpec(memory_space=pl.ANY)] * 5,
            out_specs=vmem,
            scratch_shapes=[
                pltpu.VMEM((32, 2, 128, 128), f32),
                pltpu.VMEM((8, 8), jnp.int32),
                pltpu.VMEM((4, 8, 128), jnp.int32),
                pltpu.SMEM((4, 8, 128), jnp.int32),
                pltpu.VMEM((4, 8, 128), f32),
                pltpu.VMEM((16, 128), f32),
                pltpu.VMEM((2, 16, 128), f32),
                pltpu.VMEM((32, 256), jnp.bfloat16),
                pltpu.VMEM((128, 128), f32),
                pltpu.VMEM((8, 64, 128), f32),
                pltpu.VMEM((24, 128), f32),
                pltpu.VMEM((24, 128), f32),
                pltpu.VMEM((24, 128), f32),
                pltpu.VMEM((2, 4, 40, 128), f32),
                pltpu.VMEM((2, 24, 128), f32),
                pltpu.VMEM((2, 16, 128), f32),
                pltpu.VMEM((2, 16, 128), f32),
                pltpu.VMEM((2, 8, 128), f32),
                pltpu.VMEM((2, 8, 128), f32),
                pltpu.VMEM((2, 32, 1, 128), f32),
                dma, dma((2,)), pltpu.SemaphoreType.REGULAR((3,)), dma, dma((2,)), dma((2,)), dma, dma,
                dma((2,)), dma((2, CHUNKS)), dma((2,)), dma((2,)), dma((2,)), dma((2,)),
            ],
            compiler_params=pltpu.CompilerParams(collective_id=0, has_side_effects=True),
            name="pcg",
        )(jac_bus, pattern, branch_weight, bus_diag, right_side)
        before, direction, resid, along, alpha = (last[8 * k : 8 * k + 8] for k in range(5))
        return before + alpha * direction, resid - alpha * along

    axes = ("region", "blk")
    in_specs = (P("region", "blk", None, None),) + (P(axes, None),) * 4
    return jax.shard_map(
        body, mesh=mesh, in_specs=in_specs, out_specs=(P(axes, None),) * 2, check_vma=False
    )
```

```python
import jax
import jax.numpy as jnp
from jax import lax
from jax.experimental import pallas as pl
from jax.experimental.pallas import tpu as pltpu
from jax.sharding import PartitionSpec as P

ITERS = 12
EARLY = 18
EACH = 5
INTO = 1
CHUNKS = 2
SPAN = 32 // CHUNKS
MESH = pl.DeviceIdType.MESH


def farness(offset):
    steps = [min(n, 4 - n) for n in offset[:2]]
    return (min(steps) > 0, sum(steps), offset[2] == 0)


def kernel(
    n_reg, n_blk,
    jac_hbm, pattern_hbm, weight_hbm, diag_hbm, rhs_hbm,
    out_ref,
    jac, pat, pv, psm, wv, hsend, hbuf, oht, stage, part, uv, qv, diag, xbuf, csend, rlo16, rhi16, rlo8, rhi8, dbuf,
    jsem, isem, far_sem, psem, gsend, grecv, hsend_sem, hrecv, xsend, xrecv, rsend, rrecv, dsend, drecv,
):
    reg = lax.axis_index("region")
    blk = lax.axis_index("blk")

    def region_at(k):
        return lax.rem(reg + k + n_reg, n_reg)

    def blk_at(k):
        return lax.rem(blk + k, n_blk)

    def to_blk(k):
        return (reg, blk_at(k))

    def to_reg(k):
        return (region_at(k), blk)

    def remote(src, dst, ssem, rsem, dev):
        return pltpu.make_async_remote_copy(
            src_ref=src, dst_ref=dst, send_sem=ssem, recv_sem=rsem,
            device_id=dev, device_id_type=MESH,
        )

    jcopies = [
        pltpu.make_async_copy(jac_hbm, jac, jsem)
        for _ in range(1)
    ]
    icopies = [
        pltpu.make_async_copy(pattern_hbm, pat, isem.at[1]),
        pltpu.make_async_copy(weight_hbm, wv.at[blk], isem.at[0]),
        pltpu.make_async_copy(diag_hbm, hsend.at[pl.ds(0, 8)], isem.at[0]),
        pltpu.make_async_copy(rhs_hbm, hsend.at[pl.ds(8, 8)], isem.at[0]),
    ]
    for c in icopies + jcopies:
        c.start()

    barrier = pltpu.get_barrier_semaphore()
    near = [to_blk(k) for k in range(1, n_blk)] + [to_reg(k) for k in (1, -1, 2, -2)]
    for dev in near:
        pl.semaphore_signal(barrier, inc=1, device_id=dev, device_id_type=MESH)

    def far_signal(n):
        for k in (2 << n, -(2 << n)):
            pl.semaphore_signal(far_sem.at[n], inc=1, device_id=to_reg(k), device_id_type=MESH)

    pv[blk] = jnp.zeros((8, 128), jnp.int32)
    icopies[0].wait()
    landed = stage.at[pl.ds(0, 24)]
    pltpu.make_async_copy(landed, landed, isem.at[0]).wait()
    pv[blk, :, 0:8] = pat[...]
    pl.semaphore_wait(barrier, len(near))

    gcopies = []
    for k in range(1, n_blk):
        gcopies.append(remote(pv.at[blk], pv.at[blk], gsend.at[0], grecv.at[0], to_blk(k)))
        gcopies.append(remote(wv.at[blk], wv.at[blk], gsend.at[1], grecv.at[1], to_blk(k)))
    hcopies = [
        remote(hsend, hbuf.at[0], hsend_sem, hrecv, to_reg(1)),
        remote(hsend, hbuf.at[1], hsend_sem, hrecv, to_reg(-1)),
    ]
    for c in gcopies + hcopies:
        c.start()

    def whole(ref, ssem, rsem):
        return remote(ref, ref, ssem, rsem, to_blk(1))

    gcopies = [
        whole(pv.at[pl.ds(0, n_blk - 1)], gsend.at[0], grecv.at[0]),
        whole(wv.at[pl.ds(0, n_blk - 1)], gsend.at[1], grecv.at[1]),
    ]
    hcopies = [whole(hbuf, hsend_sem, hrecv)]
    far_signal(0)
    pl.semaphore_wait(far_sem.at[0], 2)
    far_signal(1)
    for c in gcopies:
        c.wait_recv()
    pcopy = pltpu.make_async_copy(pv, psm, psem)
    pcopy.start()

    patf = pv[...].astype(jnp.float32).reshape(32, 128)
    lanes32 = lax.broadcasted_iota(jnp.int32, (32, 128), 1)
    for j in range(2):
        col = jnp.sum(jnp.where(lanes32 == 2 * blk + j, patf, 0.0), axis=1, keepdims=True)
        hit = jnp.where(lanes32.astype(jnp.float32) == col, 1.0, 0.0)
        stage[32 * j : 32 * j + 32] = hit
        stage[64 + 32 * j : 96 + 32 * j] = hit
    hot = stage[...].T[0:32]
    oht[:, 0:128] = hot.astype(jnp.bfloat16)
    oht[:, 128:256] = jnp.where(lanes32 < 64, hot, 0.0).astype(jnp.bfloat16)
    weight = wv[...].reshape(32, 128)

    def eight_sums(terms):
        total = terms[0:8]
        for k in range(1, 16):
            total = total + terms[8 * k : 8 * k + 8]
        return total

    def group_rows(slot):
        total = part[slot, pl.ds(0, 8, stride=8), :]
        for k in range(1, 8):
            total = total + part[slot, pl.ds(k, 8, stride=8), :]
        return total

    def backward_tiles(first, rows, square, beside=()):
        for t in range(first, first + rows.shape[0]):
            for copy in beside[EACH * (t - first) : EACH * (t - first) + EACH]:
                copy.start()
            wc = jnp.broadcast_to(rows[t - first : t - first + 1], (128, 128)).T
            for j in range(2):
                tile = jac[t, j]
                term = tile * wc
                if square:
                    term = term * tile
                part[4 * j + t // 8, 8 * (t % 8) : 8 * (t % 8) + 8] = eight_sums(term)

    def backward_end(par):
        whole = jnp.concatenate([group_rows(k) for k in range(8)], axis=0)
        high = whole.astype(jnp.bfloat16)
        rest = whole - high.astype(jnp.float32)
        mid = rest.astype(jnp.bfloat16)
        low = (rest - mid.astype(jnp.float32)).astype(jnp.bfloat16)
        stack = jnp.concatenate([high, mid, low, jnp.zeros((64, 128), jnp.bfloat16)], axis=0)
        total = jnp.dot(oht[...], stack, preferred_element_type=jnp.float32)
        csend[par] = total[0:24]

    def r_copies(par):
        return [
            remote(csend.at[par, pl.ds(16, 8)], rlo8.at[par], rsend.at[par], rrecv.at[par], to_reg(2)),
            remote(csend.at[par, pl.ds(0, 8)], rhi8.at[par], rsend.at[par], rrecv.at[par], to_reg(-2)),
            remote(csend.at[par, pl.ds(8, 16)], rlo16.at[par], rsend.at[par], rrecv.at[par], to_reg(1)),
            remote(csend.at[par, pl.ds(0, 16)], rhi16.at[par], rsend.at[par], rrecv.at[par], to_reg(-1)),
        ]

    def r_whole(par):
        return whole(xbuf.at[par, pl.ds(0, 2), pl.ds(0, 24)], rsend.at[par], rrecv.at[par])

    def r_sum(par):
        before = rlo8[par] + rlo16[par, 0:8] + csend[par, 0:8]
        own = rlo16[par, 8:16] + csend[par, 8:16] + rhi16[par, 0:8]
        after = csend[par, 16:24] + rhi16[par, 8:16] + rhi8[par]
        return jnp.concatenate([before, own, after], axis=0)

    for c in jcopies:
        c.wait()
    backward_tiles(0, weight, True)
    backward_end(0)
    copies = r_copies(0)
    for c in copies:
        c.start()
    pl.semaphore_wait(far_sem.at[1], 2)
    far_signal(2)
    pcopy.wait()
    for c in hcopies:
        c.wait_recv()
    copies = [r_whole(0)]
    copies[0].wait_recv()
    diag[...] = jnp.concatenate([hbuf[0, 0:8], hsend[0:8], hbuf[1, 0:8]], axis=0)
    resid0 = jnp.concatenate([hbuf[0, 8:16], hsend[8:16], hbuf[1, 8:16]], axis=0)
    inv = 1.0 / (diag[...] + r_sum(0))
    for c in copies + gcopies + hcopies:
        c.wait_send()
    pl.semaphore_wait(far_sem.at[2], 2)

    offsets = [(z, y, c) for z in range(n_reg // 8) for y in range(4) for c in range(2)][1:]
    order = sorted(offsets, key=farness, reverse=True)

    def to_offset(offset):
        z, y, c = offset
        there_z = lax.rem(reg // 8 + z, n_reg // 8)
        there_y = lax.rem(lax.rem(reg // 2, 4) + y, 4)
        return ((there_z * 4 + there_y) * 2 + lax.rem(reg + c, 2), blk)

    zeros8 = jnp.zeros((8, 128), jnp.float32)
    zeros24 = jnp.zeros((24, 128), jnp.float32)
    none = jnp.zeros((1, 1), jnp.float32)

    def forward_tiles(source_ref, c, before=()):
        for t in range(SPAN * c, SPAN * c + SPAN):
            if t == SPAN * c + INTO:
                for copy in before:
                    copy.start()
            x0 = source_ref[pl.ds(psm[t // 8, t % 8, 2 * blk], 1), :]
            x1 = source_ref[pl.ds(psm[t // 8, t % 8, 2 * blk + 1], 1), :]
            both = jac[t, 0] * x0 + jac[t, 1] * x1
            part[t // 8, 8 * (t % 8) : 8 * (t % 8) + 8] = eight_sums(both.T)
        return jnp.concatenate([group_rows(SPAN // 8 * c + g) for g in range(SPAN // 8)], axis=0)

    def chunk_at(c):
        return SPAN * c + (8 if c else 0)

    def place(par, c, rows):
        xbuf[par, blk, chunk_at(c) : chunk_at(c) + SPAN] = rows
        mine = xbuf.at[par, blk, pl.ds(chunk_at(c), SPAN if c else SPAN + 2)]
        return [remote(mine, mine, xsend.at[par], xrecv.at[par, c], to_blk(k)) for k in (2, 1, 3)]

    def place_sums(par, own_u, own_r):
        first = jnp.sum(own_u * own_r, axis=0, keepdims=True)
        second = jnp.sum(own_u * own_u * diag[8:16], axis=0, keepdims=True)
        xbuf[par, blk, SPAN : SPAN + 1] = first
        xbuf[par, blk, SPAN + 1 : SPAN + 2] = second

    def bus_sums(par, rpar, wide):
        energy = jnp.zeros((1, 128), jnp.float32)
        low_lanes = lax.broadcasted_iota(jnp.int32, (1, 128), 1) < 64
        for c in range(CHUNKS):
            at = chunk_at(c)
            landed = xbuf.at[par, pl.ds(0, n_blk - 1), pl.ds(at, SPAN if c else SPAN + 2)]
            whole(landed, xsend.at[par], xrecv.at[par, c]).wait_recv()
            b0, b1, b2, b3 = (xbuf[par, b, at : at + (SPAN if c else SPAN + 2)] for b in range(4))
            rows = b0[:SPAN] + b1[:SPAN] + b2[:SPAN] + b3[:SPAN]
            weighted = weight[SPAN * c : SPAN * c + SPAN] * rows
            energy = energy + jnp.sum(weighted * rows, axis=0, keepdims=True)
            if c == 0:
                first = b0[SPAN:] + b1[SPAN:] + b2[SPAN:] + b3[SPAN:]
                first = first + pltpu.roll(first, 64, 1)
                held = jnp.where(low_lanes, first[0:1], first[1:2])
            if c < CHUNKS - 1:
                backward_tiles(SPAN * c, weighted, False)
        dbuf[par, reg] = held + jnp.where(low_lanes, 0.0, energy + pltpu.roll(energy, 64, 1))
        dcopies = [
            remote(dbuf.at[par, reg], dbuf.at[par, reg], dsend.at[par], drecv.at[par], to_offset(k))
            for k in order
        ]
        backward_tiles(32 - SPAN, weighted, False, dcopies[:EARLY])
        backward_end(rpar)
        for c in r_copies(rpar)[0 if wide else 2 :] + dcopies[EARLY:]:
            c.start()
        others = dbuf.at[par, pl.ds(0, n_reg - 1)]
        return whole(others, dsend.at[par], drecv.at[par])

    def scalars(par, over_gamma, over_alpha):
        sums = jnp.sum(dbuf[par], axis=0)
        low_lanes = lax.broadcasted_iota(jnp.int32, (1, 128), 1) < 64
        gamma = jnp.sum(jnp.where(low_lanes, sums, 0.0), axis=1, keepdims=True)
        delta = jnp.sum(jnp.where(low_lanes, 0.0, sums), axis=1, keepdims=True)
        beta = gamma * over_gamma
        alpha = gamma / (delta - beta * gamma * over_alpha)
        return gamma, alpha, beta

    def sent_whole(par):
        sent = xbuf.at[par, pl.ds(0, n_blk - 1), pl.ds(0, 34)]
        return whole(sent, xsend.at[par], xrecv.at[par, 0])

    uv[0:24] = inv * resid0
    uv[24:32] = zeros8
    qv[24:32] = zeros8
    place_sums(0, uv[8:16], resid0[8:16])
    for c in range(CHUNKS):
        for copy in place(0, c, forward_tiles(uv, c)):
            copy.start()

    def step(i, carry):
        solution, direction, resid, along, over_gamma, over_alpha = carry
        par = lax.rem(i, 2)
        rpar = lax.rem(i + 1, 2)
        scaled = inv * resid
        uv[0:24] = scaled
        qv[0:24] = inv * along
        dall = bus_sums(par, rpar, True)
        kept_u = [forward_tiles(uv, c) for c in range(CHUNKS)]
        kept_q = [forward_tiles(qv, c) for c in range(CHUNKS)]
        rall = r_whole(rpar)
        rall.wait_recv()
        image = diag[...] * scaled + r_sum(rpar)
        uv[0:24] = inv * image
        fresh = forward_tiles(uv, 0)
        dall.wait_recv()
        gamma, alpha, beta = scalars(par, over_gamma, over_alpha)
        direction = scaled[8:16] + beta * direction
        along = image + beta * along
        solution = solution + alpha * direction
        resid = resid - alpha * along
        place_sums(rpar, inv[8:16] * resid[8:16], resid[8:16])
        copies = place(rpar, 0, kept_u[0] - alpha * (fresh + beta * kept_q[0]))
        for c in range(1, CHUNKS):
            fresh = forward_tiles(uv, c, copies)
            copies = place(rpar, c, kept_u[c] - alpha * (fresh + beta * kept_q[c]))
        for copy in copies:
            copy.start()
        for c in (sent_whole(par), rall, dall):
            c.wait_send()
        return (solution, direction, resid, along, 1.0 / gamma, 1.0 / alpha)

    carry = lax.fori_loop(0, ITERS - 1, step, (zeros8, zeros8, resid0, zeros24, none, none))
    solution, direction, resid, along, over_gamma, over_alpha = carry
    par, rpar = (ITERS - 1) % 2, ITERS % 2
    dall = bus_sums(par, rpar, False)
    rall = whole(xbuf.at[rpar, pl.ds(0, 2), pl.ds(0, 16)], rsend.at[rpar], rrecv.at[rpar])
    rall.wait_recv()
    scaled = inv[8:16] * resid[8:16]
    image = diag[8:16] * scaled + (rlo16[rpar, 8:16] + csend[rpar, 8:16] + rhi16[rpar, 0:8])
    dall.wait_recv()
    gamma, alpha, beta = scalars(par, over_gamma, over_alpha)
    out_ref[0:8] = solution
    out_ref[8:16] = scaled + beta * direction
    out_ref[16:24] = resid[8:16]
    out_ref[24:32] = image + beta * along[8:16]
    out_ref[32:40] = jnp.broadcast_to(alpha, (8, 128))
    for c in (sent_whole(par), rall, dall):
        c.wait_send()


def solution(mesh):
    n_reg, n_blk = mesh.shape["region"], mesh.shape["blk"]
    f32 = jnp.float32

    def body(jac_bus, pattern, branch_weight, bus_diag, right_side):
        vmem = pl.BlockSpec(memory_space=pltpu.VMEM)
        shape = jax.ShapeDtypeStruct((40, 128), f32)
        dma = pltpu.SemaphoreType.DMA

        def call(*args):
            return kernel(n_reg, n_blk, *args)

        last = pl.pallas_call(
            call,
            out_shape=shape,
            in_specs=[pl.BlockSpec(memory_space=pl.ANY)] * 5,
            out_specs=vmem,
            scratch_shapes=[
                pltpu.VMEM((32, 2, 128, 128), f32),
                pltpu.VMEM((8, 8), jnp.int32),
                pltpu.VMEM((4, 8, 128), jnp.int32),
                pltpu.SMEM((4, 8, 128), jnp.int32),
                pltpu.VMEM((4, 8, 128), f32),
                pltpu.VMEM((16, 128), f32),
                pltpu.VMEM((2, 16, 128), f32),
                pltpu.VMEM((32, 256), jnp.bfloat16),
                pltpu.VMEM((128, 128), f32),
                pltpu.VMEM((8, 72, 128), f32),
                pltpu.VMEM((32, 128), f32),
                pltpu.VMEM((32, 128), f32),
                pltpu.VMEM((24, 128), f32),
                pltpu.VMEM((2, 4, 40, 128), f32),
                pltpu.VMEM((2, 24, 128), f32),
                pltpu.VMEM((2, 16, 128), f32),
                pltpu.VMEM((2, 16, 128), f32),
                pltpu.VMEM((2, 8, 128), f32),
                pltpu.VMEM((2, 8, 128), f32),
                pltpu.VMEM((2, 32, 1, 128), f32),
                dma, dma((2,)), pltpu.SemaphoreType.REGULAR((3,)), dma, dma((2,)), dma((2,)), dma, dma,
                dma((2,)), dma((2, CHUNKS)), dma((2,)), dma((2,)), dma((2,)), dma((2,)),
            ],
            compiler_params=pltpu.CompilerParams(collective_id=0, has_side_effects=True),
            name="pcg",
        )(jac_bus, pattern, branch_weight, bus_diag, right_side)
        before, direction, resid, along, alpha = (last[8 * k : 8 * k + 8] for k in range(5))
        return before + alpha * direction, resid - alpha * along

    axes = ("region", "blk")
    in_specs = (P("region", "blk", None, None),) + (P(axes, None),) * 4
    return jax.shard_map(
        body, mesh=mesh, in_specs=in_specs, out_specs=(P(axes, None),) * 2, check_vma=False
    )
```

```python
import jax
import jax.numpy as jnp
from jax import lax
from jax.experimental import pallas as pl
from jax.experimental.pallas import tpu as pltpu
from jax.sharding import PartitionSpec as P

ITERS = 12
EARLY = 18
EACH = 5
INTO = 1
CHUNKS = 2
SPAN = 32 // CHUNKS
MESH = pl.DeviceIdType.MESH


def farness(offset):
    steps = [min(n, 4 - n) for n in offset[:2]]
    return (min(steps) > 0, sum(steps), offset[2] == 0)


def kernel(
    n_reg, n_blk,
    jac_hbm, pattern_hbm, weight_hbm, diag_hbm, rhs_hbm,
    out_ref,
    jac, pat, pv, psm, wv, hsend, hbuf, oht, stage, part, uv, qv, diag, xbuf, csend, rlo16, rhi16, rlo8, rhi8, dbuf,
    jsem, isem, far_sem, psem, gsend, grecv, hsend_sem, hrecv, xsend, xrecv, rsend, rrecv, dsend, drecv,
):
    reg = lax.axis_index("region")
    blk = lax.axis_index("blk")

    def region_at(k):
        return lax.rem(reg + k + n_reg, n_reg)

    def blk_at(k):
        return lax.rem(blk + k, n_blk)

    def to_blk(k):
        return (reg, blk_at(k))

    def to_reg(k):
        return (region_at(k), blk)

    def remote(src, dst, ssem, rsem, dev):
        return pltpu.make_async_remote_copy(
            src_ref=src, dst_ref=dst, send_sem=ssem, recv_sem=rsem,
            device_id=dev, device_id_type=MESH,
        )

    jcopies = [
        pltpu.make_async_copy(jac_hbm, jac, jsem)
        for _ in range(1)
    ]
    icopies = [
        pltpu.make_async_copy(pattern_hbm, pat, isem.at[1]),
        pltpu.make_async_copy(weight_hbm, wv.at[blk], isem.at[0]),
        pltpu.make_async_copy(diag_hbm, hsend.at[pl.ds(0, 8)], isem.at[0]),
        pltpu.make_async_copy(rhs_hbm, hsend.at[pl.ds(8, 8)], isem.at[0]),
    ]
    for c in icopies + jcopies:
        c.start()

    barrier = pltpu.get_barrier_semaphore()
    near = [to_blk(k) for k in range(1, n_blk)] + [to_reg(k) for k in (1, -1, 2, -2)]
    for dev in near:
        pl.semaphore_signal(barrier, inc=1, device_id=dev, device_id_type=MESH)

    def far_signal(n):
        for k in (2 << n, -(2 << n)):
            pl.semaphore_signal(far_sem.at[n], inc=1, device_id=to_reg(k), device_id_type=MESH)

    pv[blk] = jnp.zeros((8, 128), jnp.int32)
    icopies[0].wait()
    landed = stage.at[pl.ds(0, 24)]
    pltpu.make_async_copy(landed, landed, isem.at[0]).wait()
    pv[blk, :, 0:8] = pat[...]
    pl.semaphore_wait(barrier, len(near))

    gcopies = []
    for k in range(1, n_blk):
        gcopies.append(remote(pv.at[blk], pv.at[blk], gsend.at[0], grecv.at[0], to_blk(k)))
        gcopies.append(remote(wv.at[blk], wv.at[blk], gsend.at[1], grecv.at[1], to_blk(k)))
    hcopies = [
        remote(hsend, hbuf.at[0], hsend_sem, hrecv, to_reg(1)),
        remote(hsend, hbuf.at[1], hsend_sem, hrecv, to_reg(-1)),
    ]
    for c in gcopies + hcopies:
        c.start()

    def whole(ref, ssem, rsem):
        return remote(ref, ref, ssem, rsem, to_blk(1))

    gcopies = [
        whole(pv.at[pl.ds(0, n_blk - 1)], gsend.at[0], grecv.at[0]),
        whole(wv.at[pl.ds(0, n_blk - 1)], gsend.at[1], grecv.at[1]),
    ]
    hcopies = [whole(hbuf, hsend_sem, hrecv)]
    far_signal(0)
    pl.semaphore_wait(far_sem.at[0], 2)
    far_signal(1)
    for c in gcopies:
        c.wait_recv()
    pcopy = pltpu.make_async_copy(pv, psm, psem)
    pcopy.start()

    patf = pv[...].astype(jnp.float32).reshape(32, 128)
    lanes32 = lax.broadcasted_iota(jnp.int32, (32, 128), 1)
    for j in range(2):
        col = jnp.sum(jnp.where(lanes32 == 2 * blk + j, patf, 0.0), axis=1, keepdims=True)
        hit = jnp.where(lanes32.astype(jnp.float32) == col, 1.0, 0.0)
        stage[32 * j : 32 * j + 32] = hit
        stage[64 + 32 * j : 96 + 32 * j] = hit
    hot = stage[...].T[0:32]
    oht[:, 0:128] = hot.astype(jnp.bfloat16)
    oht[:, 128:256] = jnp.where(lanes32 < 64, hot, 0.0).astype(jnp.bfloat16)
    weight = wv[...].reshape(32, 128)

    def eight_sums(terms):
        total = terms[0:8]
        for k in range(1, 16):
            total = total + terms[8 * k : 8 * k + 8]
        return total

    def group_rows(slot):
        total = part[slot, pl.ds(0, 8, stride=8), :]
        for k in range(1, 8):
            total = total + part[slot, pl.ds(k, 8, stride=8), :]
        return total

    def backward_tiles(first, rows, square, beside=()):
        for t in range(first, first + rows.shape[0]):
            for copy in beside[EACH * (t - first) : EACH * (t - first) + EACH]:
                copy.start()
            wc = jnp.broadcast_to(rows[t - first : t - first + 1], (128, 128)).T
            for j in range(2):
                tile = jac[t, j]
                term = tile * wc
                if square:
                    term = term * tile
                part[4 * j + t // 8, 8 * (t % 8) : 8 * (t % 8) + 8] = eight_sums(term)

    def backward_end(par):
        whole = jnp.concatenate([group_rows(k) for k in range(8)], axis=0)
        high = whole.astype(jnp.bfloat16)
        mid = (whole - high.astype(jnp.float32)).astype(jnp.bfloat16)
        stack = jnp.concatenate([high, mid], axis=0)
        total = jnp.dot(oht[:, 0:128], stack, preferred_element_type=jnp.float32)
        csend[par] = total[0:24]

    def r_copies(par):
        return [
            remote(csend.at[par, pl.ds(16, 8)], rlo8.at[par], rsend.at[par], rrecv.at[par], to_reg(2)),
            remote(csend.at[par, pl.ds(0, 8)], rhi8.at[par], rsend.at[par], rrecv.at[par], to_reg(-2)),
            remote(csend.at[par, pl.ds(8, 16)], rlo16.at[par], rsend.at[par], rrecv.at[par], to_reg(1)),
            remote(csend.at[par, pl.ds(0, 16)], rhi16.at[par], rsend.at[par], rrecv.at[par], to_reg(-1)),
        ]

    def r_whole(par):
        return whole(xbuf.at[par, pl.ds(0, 2), pl.ds(0, 24)], rsend.at[par], rrecv.at[par])

    def r_sum(par):
        before = rlo8[par] + rlo16[par, 0:8] + csend[par, 0:8]
        own = rlo16[par, 8:16] + csend[par, 8:16] + rhi16[par, 0:8]
        after = csend[par, 16:24] + rhi16[par, 8:16] + rhi8[par]
        return jnp.concatenate([before, own, after], axis=0)

    for c in jcopies:
        c.wait()
    backward_tiles(0, weight, True)
    backward_end(0)
    copies = r_copies(0)
    for c in copies:
        c.start()
    pl.semaphore_wait(far_sem.at[1], 2)
    far_signal(2)
    pcopy.wait()
    for c in hcopies:
        c.wait_recv()
    copies = [r_whole(0)]
    copies[0].wait_recv()
    diag[...] = jnp.concatenate([hbuf[0, 0:8], hsend[0:8], hbuf[1, 0:8]], axis=0)
    resid0 = jnp.concatenate([hbuf[0, 8:16], hsend[8:16], hbuf[1, 8:16]], axis=0)
    inv = 1.0 / (diag[...] + r_sum(0))
    for c in copies + gcopies + hcopies:
        c.wait_send()
    pl.semaphore_wait(far_sem.at[2], 2)

    offsets = [(z, y, c) for z in range(n_reg // 8) for y in range(4) for c in range(2)][1:]
    order = sorted(offsets, key=farness, reverse=True)

    def to_offset(offset):
        z, y, c = offset
        there_z = lax.rem(reg // 8 + z, n_reg // 8)
        there_y = lax.rem(lax.rem(reg // 2, 4) + y, 4)
        return ((there_z * 4 + there_y) * 2 + lax.rem(reg + c, 2), blk)

    zeros8 = jnp.zeros((8, 128), jnp.float32)
    zeros24 = jnp.zeros((24, 128), jnp.float32)
    none = jnp.zeros((1, 1), jnp.float32)

    def forward_tiles(source_ref, c, before=()):
        for t in range(SPAN * c, SPAN * c + SPAN):
            if t == SPAN * c + INTO:
                for copy in before:
                    copy.start()
            x0 = source_ref[pl.ds(psm[t // 8, t % 8, 2 * blk], 1), :]
            x1 = source_ref[pl.ds(psm[t // 8, t % 8, 2 * blk + 1], 1), :]
            both = jac[t, 0] * x0 + jac[t, 1] * x1
            part[t // 8, 8 * (t % 8) : 8 * (t % 8) + 8] = eight_sums(both.T)
        return jnp.concatenate([group_rows(SPAN // 8 * c + g) for g in range(SPAN // 8)], axis=0)

    def chunk_at(c):
        return SPAN * c + (8 if c else 0)

    def place(par, c, rows):
        xbuf[par, blk, chunk_at(c) : chunk_at(c) + SPAN] = rows
        mine = xbuf.at[par, blk, pl.ds(chunk_at(c), SPAN if c else SPAN + 2)]
        return [remote(mine, mine, xsend.at[par], xrecv.at[par, c], to_blk(k)) for k in (2, 1, 3)]

    def place_sums(par, own_u, own_r):
        first = jnp.sum(own_u * own_r, axis=0, keepdims=True)
        second = jnp.sum(own_u * own_u * diag[8:16], axis=0, keepdims=True)
        xbuf[par, blk, SPAN : SPAN + 1] = first
        xbuf[par, blk, SPAN + 1 : SPAN + 2] = second

    def bus_sums(par, rpar, wide):
        energy = jnp.zeros((1, 128), jnp.float32)
        low_lanes = lax.broadcasted_iota(jnp.int32, (1, 128), 1) < 64
        for c in range(CHUNKS):
            at = chunk_at(c)
            landed = xbuf.at[par, pl.ds(0, n_blk - 1), pl.ds(at, SPAN if c else SPAN + 2)]
            whole(landed, xsend.at[par], xrecv.at[par, c]).wait_recv()
            b0, b1, b2, b3 = (xbuf[par, b, at : at + (SPAN if c else SPAN + 2)] for b in range(4))
            rows = b0[:SPAN] + b1[:SPAN] + b2[:SPAN] + b3[:SPAN]
            weighted = weight[SPAN * c : SPAN * c + SPAN] * rows
            energy = energy + jnp.sum(weighted * rows, axis=0, keepdims=True)
            if c == 0:
                first = b0[SPAN:] + b1[SPAN:] + b2[SPAN:] + b3[SPAN:]
                first = first + pltpu.roll(first, 64, 1)
                held = jnp.where(low_lanes, first[0:1], first[1:2])
            if c < CHUNKS - 1:
                backward_tiles(SPAN * c, weighted, False)
        dbuf[par, reg] = held + jnp.where(low_lanes, 0.0, energy + pltpu.roll(energy, 64, 1))
        dcopies = [
            remote(dbuf.at[par, reg], dbuf.at[par, reg], dsend.at[par], drecv.at[par], to_offset(k))
            for k in order
        ]
        backward_tiles(32 - SPAN, weighted, False, dcopies[:EARLY])
        backward_end(rpar)
        for c in r_copies(rpar)[0 if wide else 2 :] + dcopies[EARLY:]:
            c.start()
        others = dbuf.at[par, pl.ds(0, n_reg - 1)]
        return whole(others, dsend.at[par], drecv.at[par])

    def scalars(par, over_gamma, over_alpha):
        sums = jnp.sum(dbuf[par], axis=0)
        low_lanes = lax.broadcasted_iota(jnp.int32, (1, 128), 1) < 64
        gamma = jnp.sum(jnp.where(low_lanes, sums, 0.0), axis=1, keepdims=True)
        delta = jnp.sum(jnp.where(low_lanes, 0.0, sums), axis=1, keepdims=True)
        beta = gamma * over_gamma
        alpha = gamma / (delta - beta * gamma * over_alpha)
        return gamma, alpha, beta

    def sent_whole(par):
        sent = xbuf.at[par, pl.ds(0, n_blk - 1), pl.ds(0, 34)]
        return whole(sent, xsend.at[par], xrecv.at[par, 0])

    uv[0:24] = inv * resid0
    uv[24:32] = zeros8
    qv[24:32] = zeros8
    place_sums(0, uv[8:16], resid0[8:16])
    for c in range(CHUNKS):
        for copy in place(0, c, forward_tiles(uv, c)):
            copy.start()

    def step(i, carry):
        solution, direction, resid, along, over_gamma, over_alpha = carry
        par = lax.rem(i, 2)
        rpar = lax.rem(i + 1, 2)
        scaled = inv * resid
        uv[0:24] = scaled
        qv[0:24] = inv * along
        dall = bus_sums(par, rpar, True)
        kept_u = [forward_tiles(uv, c) for c in range(CHUNKS)]
        kept_q = [forward_tiles(qv, c) for c in range(CHUNKS)]
        rall = r_whole(rpar)
        rall.wait_recv()
        image = diag[...] * scaled + r_sum(rpar)
        uv[0:24] = inv * image
        fresh = forward_tiles(uv, 0)
        dall.wait_recv()
        gamma, alpha, beta = scalars(par, over_gamma, over_alpha)
        direction = scaled[8:16] + beta * direction
        along = image + beta * along
        solution = solution + alpha * direction
        resid = resid - alpha * along
        place_sums(rpar, inv[8:16] * resid[8:16], resid[8:16])
        copies = place(rpar, 0, kept_u[0] - alpha * (fresh + beta * kept_q[0]))
        for c in range(1, CHUNKS):
            fresh = forward_tiles(uv, c, copies)
            copies = place(rpar, c, kept_u[c] - alpha * (fresh + beta * kept_q[c]))
        for copy in copies:
            copy.start()
        for c in (sent_whole(par), rall, dall):
            c.wait_send()
        return (solution, direction, resid, along, 1.0 / gamma, 1.0 / alpha)

    carry = lax.fori_loop(0, ITERS - 1, step, (zeros8, zeros8, resid0, zeros24, none, none))
    solution, direction, resid, along, over_gamma, over_alpha = carry
    par, rpar = (ITERS - 1) % 2, ITERS % 2
    dall = bus_sums(par, rpar, False)
    rall = whole(xbuf.at[rpar, pl.ds(0, 2), pl.ds(0, 16)], rsend.at[rpar], rrecv.at[rpar])
    rall.wait_recv()
    scaled = inv[8:16] * resid[8:16]
    image = diag[8:16] * scaled + (rlo16[rpar, 8:16] + csend[rpar, 8:16] + rhi16[rpar, 0:8])
    dall.wait_recv()
    gamma, alpha, beta = scalars(par, over_gamma, over_alpha)
    out_ref[0:8] = solution
    out_ref[8:16] = scaled + beta * direction
    out_ref[16:24] = resid[8:16]
    out_ref[24:32] = image + beta * along[8:16]
    out_ref[32:40] = jnp.broadcast_to(alpha, (8, 128))
    for c in (sent_whole(par), rall, dall):
        c.wait_send()


def solution(mesh):
    n_reg, n_blk = mesh.shape["region"], mesh.shape["blk"]
    f32 = jnp.float32

    def body(jac_bus, pattern, branch_weight, bus_diag, right_side):
        vmem = pl.BlockSpec(memory_space=pltpu.VMEM)
        shape = jax.ShapeDtypeStruct((40, 128), f32)
        dma = pltpu.SemaphoreType.DMA

        def call(*args):
            return kernel(n_reg, n_blk, *args)

        last = pl.pallas_call(
            call,
            out_shape=shape,
            in_specs=[pl.BlockSpec(memory_space=pl.ANY)] * 5,
            out_specs=vmem,
            scratch_shapes=[
                pltpu.VMEM((32, 2, 128, 128), f32),
                pltpu.VMEM((8, 8), jnp.int32),
                pltpu.VMEM((4, 8, 128), jnp.int32),
                pltpu.SMEM((4, 8, 128), jnp.int32),
                pltpu.VMEM((4, 8, 128), f32),
                pltpu.VMEM((16, 128), f32),
                pltpu.VMEM((2, 16, 128), f32),
                pltpu.VMEM((32, 256), jnp.bfloat16),
                pltpu.VMEM((128, 128), f32),
                pltpu.VMEM((8, 72, 128), f32),
                pltpu.VMEM((32, 128), f32),
                pltpu.VMEM((32, 128), f32),
                pltpu.VMEM((24, 128), f32),
                pltpu.VMEM((2, 4, 40, 128), f32),
                pltpu.VMEM((2, 24, 128), f32),
                pltpu.VMEM((2, 16, 128), f32),
                pltpu.VMEM((2, 16, 128), f32),
                pltpu.VMEM((2, 8, 128), f32),
                pltpu.VMEM((2, 8, 128), f32),
                pltpu.VMEM((2, 32, 1, 128), f32),
                dma, dma((2,)), pltpu.SemaphoreType.REGULAR((3,)), dma, dma((2,)), dma((2,)), dma, dma,
                dma((2,)), dma((2, CHUNKS)), dma((2,)), dma((2,)), dma((2,)), dma((2,)),
            ],
            compiler_params=pltpu.CompilerParams(collective_id=0, has_side_effects=True),
            name="pcg",
        )(jac_bus, pattern, branch_weight, bus_diag, right_side)
        before, direction, resid, along, alpha = (last[8 * k : 8 * k + 8] for k in range(5))
        return before + alpha * direction, resid - alpha * along

    axes = ("region", "blk")
    in_specs = (P("region", "blk", None, None),) + (P(axes, None),) * 4
    return jax.shard_map(
        body, mesh=mesh, in_specs=in_specs, out_specs=(P(axes, None),) * 2, check_vma=False
    )
```
